256 devices in a mesh: dp: 8 (over z), mp: 32 (over y, x, core).
Axes of the slice: x: 4, y: 4, z: 8, core: 2. Of those that a mesh axis runs over, the one named last changes fastest.
Arguments:
- tokens: bfloat16 [16384, 16384], P('dp', 'mp'), may hold values from -6 to 6
- inner_one: bfloat16 [128, 128, 128], P('mp'), may hold values from -0.5 to 0.5
- outer_one: bfloat16 [128, 128, 128], P('mp'), may hold values from -0.5 to 0.5
- inner_two: bfloat16 [128, 128, 128], P('mp'), may hold values from -0.5 to 0.5
- outer_two: bfloat16 [128, 128, 128], P('mp'), may hold values from -0.5 to 0.5
- cotangent: bfloat16 [16384, 16384], P('dp', 'mp'), may hold values from -6 to 6
Outputs:
- output: bfloat16 [16384, 16384], P('dp', 'mp')
- input_grad: bfloat16 [16384, 16384], P('dp', 'mp')
- inner_one_grad: float32 [128, 128, 128], P('mp', 'dp')
- outer_one_grad: float32 [128, 128, 128], P('mp', 'dp')
- inner_two_grad: float32 [128, 128, 128], P('mp', 'dp')
- outer_two_grad: float32 [128, 128, 128], P('mp', 'dp')
The draws below stay inside these ranges and needn't reach their ends.
All inputs are finite; a program needn't handle non-finite values.
Results may differ from the reference program's by a relative error of at most 0.0069.
Values may be sent and summed in bfloat16 or wider, within the bound.
No kernel may reach another device: no remote copies, remote signals or barrier semaphores. Data moves between devices by JAX's collectives and lax.ppermute only.
A program may use at most 128 MiB of HBM per device.

```python
from functools import partial
import jax
import jax.numpy as jnp
from jax import lax

NB = 128
TOK_DEV = 2048
D = 16384
TOKENS = 16384
N_DP = 8


def block_scale(stream_key, extent, cuts, least, top_value):
    gain = 1.0
    for axis_at, shards_of in cuts:
        heights = jax.random.uniform(jax.random.fold_in(jax.random.fold_in(stream_key, 6), axis_at), (shards_of,), jnp.float32, least / len(cuts), top_value / len(cuts))
        gain = gain * jnp.repeat(jnp.exp(heights), extent[axis_at] // shards_of).reshape((-1,) + (1,) * (len(extent) - 1 - axis_at))
    return gain


def noise(key, shape, scale, bound, cuts=(), kind=jnp.bfloat16):
    array = scale * jax.random.normal(key, shape, jnp.float32)
    if cuts:
        array = array * block_scale(key, shape, cuts, -0.22, 0.18)
    return jnp.clip(array, -bound, bound).astype(kind)


def setup_inputs(seed: int = 0) -> dict:
    key_of = jax.random.split(jax.random.key(seed), 7)
    return {
        "tokens": noise(key_of[0], (TOKENS, D), 1.0, 6.0, ((0, 8), (1, 32))),
        "inner_one": noise(key_of[1], (NB, NB, NB), NB ** -0.5, 0.5, ((0, 32),)),
        "outer_one": noise(key_of[2], (NB, NB, NB), NB ** -0.5, 0.5, ((0, 32),)),
        "inner_two": noise(key_of[3], (NB, NB, NB), NB ** -0.5, 0.5, ((0, 32),)),
        "outer_two": noise(key_of[4], (NB, NB, NB), NB ** -0.5, 0.5, ((0, 32),)),
        "cotangent": noise(key_of[5], (TOKENS, D), 1.0, 6.0, ((0, 8), (1, 32))),
    }


def gelu_tanh(values):
    return jax.nn.gelu(values, approximate=True)

def rounded(values):
    return lax.optimization_barrier(values.astype(jnp.bfloat16))

def as_float(values):
    return values.astype(jnp.float32)

def one_block(weights, totals, pieces):
    x_block, g_block = pieces
    tok_rows = x_block.shape[0]
    inputs = x_block.reshape(tok_rows, NB, NB)
    grads = g_block.reshape(tok_rows, NB, NB)
    w_one, o_one, w_two, o_two = weights
    first_mid = rounded(jnp.einsum('tbk,bkj->tbj', as_float(inputs), as_float(w_one)))
    first_perm = jnp.transpose(first_mid, (0, 2, 1))
    pre_act = jnp.einsum('tjb,jbl->tjl', as_float(first_perm), as_float(o_one))
    hidden = rounded(gelu_tanh(pre_act))
    second_mid = rounded(jnp.einsum('tbk,bkj->tbj', as_float(hidden), as_float(w_two)))
    second_perm = jnp.transpose(second_mid, (0, 2, 1))
    output = jnp.einsum('tjb,jbl->tjl', as_float(second_perm), as_float(o_two)).astype(jnp.bfloat16)
    grad_perm_two = rounded(jnp.einsum('tjl,jbl->tjb', as_float(grads), as_float(o_two)))
    grad_mid_two = jnp.transpose(grad_perm_two, (0, 2, 1))
    grad_hidden = jnp.einsum('tbj,bkj->tbk', as_float(grad_mid_two), as_float(w_two))
    primal_out, pullback = jax.vjp(gelu_tanh, pre_act)
    grad_pre = rounded(pullback(grad_hidden)[0])
    grad_perm_one = rounded(jnp.einsum('tjl,jbl->tjb', as_float(grad_pre), as_float(o_one)))
    grad_mid_one = jnp.transpose(grad_perm_one, (0, 2, 1))
    input_grad = jnp.einsum('tbj,bkj->tbk', as_float(grad_mid_one), as_float(w_one)).astype(jnp.bfloat16)
    outer_two_grad = jnp.einsum('tjb,tjl->jbl', as_float(second_perm), as_float(grads))
    inner_two_grad = jnp.einsum('tbk,tbj->bkj', as_float(hidden), as_float(grad_mid_two))
    outer_one_grad = jnp.einsum('tjb,tjl->jbl', as_float(first_perm), as_float(grad_pre))
    inner_one_grad = jnp.einsum('tbk,tbj->bkj', as_float(inputs), as_float(grad_mid_one))
    new_totals = (totals[0] + inner_one_grad, totals[1] + outer_one_grad, totals[2] + inner_two_grad, totals[3] + outer_two_grad)
    return (new_totals, (output.reshape(tok_rows, D), input_grad.reshape(tok_rows, D)))

def reference(tokens, inner_one, outer_one, inner_two, outer_two, cotangent):
    weights = (inner_one, outer_one, inner_two, outer_two)
    empty = jnp.zeros((NB, NB, NB), jnp.float32)
    starts = (empty, empty, empty, empty)
    stacked = (tokens.reshape(N_DP, TOK_DEV, D), cotangent.reshape(N_DP, TOK_DEV, D))
    totals, results = lax.scan(partial(one_block, weights), starts, stacked)
    output = results[0].reshape(TOKENS, D)
    input_grad = results[1].reshape(TOKENS, D)
    return (output, input_grad, totals[0], totals[1], totals[2], totals[3])
```

```python
import jax
import jax.numpy as jnp
from jax import lax
from jax.experimental import pallas as pl
from jax.experimental.pallas import tpu as pltpu
from jax.sharding import PartitionSpec as P

BF = jnp.bfloat16
F32 = jnp.float32
GELU_SCALE = 0.7978845608028654
GELU_CUBE = 0.044715


def dot(left, right, left_dim, right_dim):
    return lax.dot_general(
        left, right, (((left_dim,), (right_dim,)), ((), ())), preferred_element_type=F32
    )


def inner_spread(block, wide, rows_wide):
    shape = (wide, 128) if rows_wide else (128, wide)
    row = lax.broadcasted_iota(jnp.int32, shape, 0)
    col = lax.broadcasted_iota(jnp.int32, shape, 1)
    hit = (row == 4 * col + block) if rows_wide else (col == 4 * row + block)
    return hit.astype(F32).astype(BF)


def outer_spread(block):
    row = lax.broadcasted_iota(jnp.int32, (512, 128), 0)
    col = lax.broadcasted_iota(jnp.int32, (512, 128), 1)
    hit = row == 16 * (col // 4) + 4 * block + col % 4
    return hit.astype(F32).astype(BF)


def fill_inner_t(weight_ref, wide_ref):
    for block in range(4):
        wide_ref[:, 128 * block:128 * block + 128] = dot(
            inner_spread(block, 512, True), weight_ref[block], 1, 1
        ).astype(BF)


def fill_inner(weight_ref, wide_ref):
    for block in range(4):
        wide_ref[128 * block:128 * block + 128, :] = dot(
            weight_ref[block], inner_spread(block, 512, False), 1, 0
        ).astype(BF)


def fill_outer(weight_ref, wide_ref):
    for block in range(4):
        wide_ref[:, 128 * block:128 * block + 128] = dot(
            outer_spread(block), weight_ref[block], 1, 0
        ).astype(BF)


def fill_outer_t(weight_ref, wide_ref):
    for block in range(4):
        wide_ref[128 * block:128 * block + 128, :] = dot(
            weight_ref[block], outer_spread(block), 0, 1
        ).astype(BF)


def first(fill):
    pl.when(pl.program_id(0) == 0)(fill)


def head_kernel(fill, x_ref, weight_ref, mid_ref, wide_ref):
    first(lambda: fill(weight_ref, wide_ref))
    mid = dot(wide_ref[...], x_ref[...], 1, 1).astype(BF)
    mid_ref[...] = mid.reshape(mid_ref.shape)


def rows(ref):
    return ref[...].reshape(512, ref.shape[-1])


def forward_kernel(perm_ref, outer_ref, inner_ref, hidden_ref, slope_ref, mid_ref, outer_wide, inner_wide):
    def fill():
        fill_outer_t(outer_ref, outer_wide)
        fill_inner_t(inner_ref, inner_wide)

    first(fill)
    pre = dot(outer_wide[...], rows(perm_ref), 1, 0)
    square = pre * pre
    bent = jnp.tanh(GELU_SCALE * (pre + GELU_CUBE * (square * pre)))
    half = 0.5 * (1.0 + bent)
    hidden = (pre * half).astype(BF)
    hidden_ref[...] = hidden
    slope_ref[...] = half + (0.5 * GELU_SCALE) * pre * (1.0 - bent * bent) * (1.0 + (3.0 * GELU_CUBE) * square)
    mid = dot(inner_wide[...], hidden, 1, 0).astype(BF)
    mid_ref[...] = mid.reshape(mid_ref.shape)


def backward_kernel(grad_mid_ref, slope_ref, inner_ref, outer_ref, grad_pre_ref, grad_perm_ref, inner_wide, outer_wide):
    def fill():
        fill_inner(inner_ref, inner_wide)
        fill_outer(outer_ref, outer_wide)

    first(fill)
    grad_hidden = dot(inner_wide[...], rows(grad_mid_ref), 1, 0)
    grad_pre = (grad_hidden * slope_ref[...]).astype(BF)
    grad_pre_ref[...] = grad_pre
    grad_perm = dot(outer_wide[...], grad_pre, 1, 0).astype(BF)
    grad_perm_ref[...] = grad_perm.reshape(grad_perm_ref.shape)


def picked(total_ref, by_j):
    row = lax.broadcasted_iota(jnp.int32, (512, 128), 0)
    mine = (row // 4) % 4 if by_j else row % 4
    value = total_ref[:, 0:128]
    for block in range(1, 4):
        value = jnp.where(mine == block, total_ref[:, 128 * block:128 * block + 128], value)
    return value


def write_outer(total_ref, picked_ref, block_ref, out_ref):
    picked_ref[...] = picked(total_ref, True)
    for j in range(4):
        for b in range(4):
            block_ref[pl.ds(b, 32, stride=4), :] = picked_ref[pl.ds(4 * j + b, 32, stride=16), :]
        for rank in range(8):
            out_ref[rank, 16 * j:16 * j + 16, :] = block_ref[16 * rank:16 * rank + 16, :].astype(out_ref.dtype)


def write_inner(total_ref, picked_ref, out_ref):
    picked_ref[...] = picked(total_ref, False)
    for b in range(4):
        block = picked_ref[pl.ds(b, 128, stride=4), :].T.astype(out_ref.dtype)
        for rank in range(8):
            out_ref[rank, 16 * b:16 * b + 16, :] = block[16 * rank:16 * rank + 16, :]


def accumulate(total_ref, value):
    step = pl.program_id(0)

    @pl.when(step == 0)
    def _():
        total_ref[...] = value

    @pl.when(step > 0)
    def _():
        total_ref[...] += value


def last(write):
    pl.when(pl.program_id(0) == pl.num_programs(0) - 1)(write)


def inner_grad_kernel(dims, grad_ref, other_ref, out_ref, total_ref, picked_ref):
    accumulate(total_ref, dot(rows(grad_ref), other_ref[...], *dims))
    last(lambda: write_inner(total_ref, picked_ref, out_ref))


def outer_grad_kernel(dims, perm_ref, other_ref, out_ref, total_ref, picked_ref, block_ref):
    accumulate(total_ref, dot(rows(perm_ref), other_ref[...], *dims))
    last(lambda: write_outer(total_ref, picked_ref, block_ref, out_ref))


def tail_kernel(fill, perm_ref, weight_ref, out_ref, wide_ref):
    first(lambda: fill(weight_ref, wide_ref))
    out_ref[...] = dot(rows(perm_ref), wide_ref[...], 0, 0).astype(BF)


def call(kernel, grid, specs, outs, scratch, args, flops, name):
    moved = sum(a.size * a.dtype.itemsize for a in args)
    moved += sum(o.size * o.dtype.itemsize for o, _ in outs)
    return pl.pallas_call(
        kernel,
        grid=(grid,),
        in_specs=specs,
        out_specs=[s for _, s in outs],
        out_shape=[o for o, _ in outs],
        scratch_shapes=scratch,
        name=name,
        cost_estimate=pl.CostEstimate(flops=flops, bytes_accessed=moved, transcendentals=0),
        compiler_params=pltpu.CompilerParams(
            dimension_semantics=("arbitrary",), vmem_limit_bytes=60 * 1024 * 1024
        ),
    )(*args)


def body(tokens, inner_one, outer_one, inner_two, outer_two, cotangent):
    tok = tokens.shape[0]
    tile = 512
    steps = tok // tile
    one = 2 * tok * 512 * 512
    shape = jax.ShapeDtypeStruct
    by_token = pl.BlockSpec((tile, 512), lambda i: (i, 0))
    by_message = pl.BlockSpec((32, 16, tile), lambda i: (0, 0, i))
    by_feature = pl.BlockSpec((512, tile), lambda i: (0, i))
    weight = pl.BlockSpec((4, 128, 128), lambda i: (0, 0, 0))
    grad_spec = pl.BlockSpec((8, 64, 128), lambda i: (0, 0, 0))
    message = shape((32, 16, tok), BF)
    feature = shape((512, tok), BF)
    token_out = shape((tok, 512), BF)
    wide = pltpu.VMEM((512, 512), BF)
    total = pltpu.VMEM((512, 512), F32)
    pick = pltpu.VMEM((512, 128), F32)
    block = pltpu.VMEM((128, 128), F32)

    def head(fill, x, w, name):
        return call(lambda *r: head_kernel(fill, *r), steps, [by_token, weight], [(message, by_message)], [wide], (x, w), one, name)[0]

    def tail(fill, perm, w, name):
        return call(lambda *r: tail_kernel(fill, *r), steps, [by_message, weight], [(token_out, by_token)], [wide], (perm, w), one, name)[0]

    def inner_grad(grad, other, spec, dims, name, kind=F32):
        return call(lambda *r: inner_grad_kernel(dims, *r), steps, [by_message, spec], [(shape((8, 64, 128), kind), grad_spec)], [total, pick], (grad, other), one, name)[0]

    def outer_grad(perm, other, spec, dims, name):
        return call(lambda *r: outer_grad_kernel(dims, *r), steps, [by_message, spec], [(shape((8, 64, 128), F32), grad_spec)], [total, pick, block], (perm, other), one, name)[0]

    def exchange(value):
        return lax.all_to_all(value, "mp", split_axis=0, concat_axis=0, tiled=True)

    def reduce(value):
        parts = lax.all_to_all(value, "dp", split_axis=0, concat_axis=0, tiled=True)
        return jnp.sum(parts.astype(F32), axis=0)

    def after(value, earlier):
        return lax.optimization_barrier((value, earlier))

    first_perm = exchange(head(fill_inner_t, tokens, inner_one, "first_mid"))
    grad_perm_two, first_perm = after(head(fill_outer, cotangent, outer_two, "grad_perm_two"), first_perm)
    grad_mid_two = exchange(grad_perm_two)
    hidden, slope, second_mid = call(
        forward_kernel, steps, [by_message, weight, weight],
        [(feature, by_feature), (shape((512, tok), F32), by_feature), (message, by_message)],
        [wide, wide], (first_perm, outer_one, inner_two), 2 * one, "hidden",
    )
    second_mid, grad_mid_two = after(second_mid, grad_mid_two)
    second_perm = exchange(second_mid)
    grad_pre, grad_perm_one = call(
        backward_kernel, steps, [by_message, by_feature, weight, weight],
        [(feature, by_feature), (message, by_message)],
        [wide, wide], (grad_mid_two, slope, inner_two, outer_one), 2 * one, "grad_pre",
    )
    grad_perm_one, second_perm = after(grad_perm_one, second_perm)
    grad_mid_one = exchange(grad_perm_one)
    inner_two_part = inner_grad(grad_mid_two, hidden, by_feature, (1, 1), "inner_two_grad")
    outer_one_part = outer_grad(first_perm, grad_pre, by_feature, (1, 1), "outer_one_grad")
    outer_two_part = outer_grad(second_perm, cotangent, by_token, (1, 0), "outer_two_grad")
    sums = jnp.concatenate([inner_two_part, outer_one_part, outer_two_part], axis=1)
    sums = lax.psum_scatter(sums, "dp", scatter_dimension=0, tiled=True).reshape(192, 128)
    output = tail(fill_outer, second_perm, outer_two, "output")
    inner_one_part = inner_grad(grad_mid_one, tokens, by_token, (1, 0), "inner_one_grad", BF)
    inner_one_sum = reduce(inner_one_part)
    input_grad = tail(fill_inner_t, grad_mid_one, inner_one, "input_grad")
    return (
        output,
        input_grad,
        inner_one_sum.reshape(4, 16, 128),
        sums[64:128].reshape(4, 16, 128),
        sums[0:64].reshape(4, 16, 128),
        sums[128:192].reshape(4, 16, 128),
    )


def solution(mesh):
    placed = (
        P("dp", "mp"),
        P("mp", None, None),
        P("mp", None, None),
        P("mp", None, None),
        P("mp", None, None),
        P("dp", "mp"),
    )
    return jax.shard_map(
        body,
        mesh=mesh,
        in_specs=placed,
        out_specs=(
            P("dp", "mp"),
            P("dp", "mp"),
            P("mp", "dp", None),
            P("mp", "dp", None),
            P("mp", "dp", None),
            P("mp", "dp", None),
        ),
        check_vma=False,
    )
```

```python
import jax
import jax.numpy as jnp
from jax import lax
from jax.experimental import pallas as pl
from jax.experimental.pallas import tpu as pltpu
from jax.sharding import PartitionSpec as P

BF = jnp.bfloat16
F32 = jnp.float32
GELU_SCALE = 0.7978845608028654
GELU_CUBE = 0.044715
TILES = 4
ROWS = 64


def dot(left, right, left_dim, right_dim):
    return lax.dot_general(
        left, right, (((left_dim,), (right_dim,)), ((), ())), preferred_element_type=F32
    )


def inner_spread(block, wide, rows_wide):
    shape = (wide, 128) if rows_wide else (128, wide)
    row = lax.broadcasted_iota(jnp.int32, shape, 0)
    col = lax.broadcasted_iota(jnp.int32, shape, 1)
    hit = (row == 4 * col + block) if rows_wide else (col == 4 * row + block)
    return hit.astype(F32).astype(BF)


def outer_spread(block):
    row = lax.broadcasted_iota(jnp.int32, (512, 128), 0)
    col = lax.broadcasted_iota(jnp.int32, (512, 128), 1)
    hit = row == 16 * (col // 4) + 4 * block + col % 4
    return hit.astype(F32).astype(BF)


def fill_inner_t(weight_ref, wide_ref):
    for block in range(4):
        wide_ref[:, 128 * block:128 * block + 128] = dot(
            inner_spread(block, 512, True), weight_ref[block], 1, 1
        ).astype(BF)


def fill_inner(weight_ref, wide_ref):
    for block in range(4):
        wide_ref[128 * block:128 * block + 128, :] = dot(
            weight_ref[block], inner_spread(block, 512, False), 1, 0
        ).astype(BF)


def fill_outer(weight_ref, wide_ref):
    for block in range(4):
        wide_ref[:, 128 * block:128 * block + 128] = dot(
            outer_spread(block), weight_ref[block], 1, 0
        ).astype(BF)


def fill_outer_t(weight_ref, wide_ref):
    for block in range(4):
        wide_ref[128 * block:128 * block + 128, :] = dot(
            weight_ref[block], outer_spread(block), 0, 1
        ).astype(BF)


def rows(value):
    return value.reshape(512, value.shape[-1])


def copies(source, target, sems, tile, axis):
    out = []
    for i in range(TILES):
        at = (slice(None),) * axis + (pl.ds(tile * i, tile),)
        out.append(pltpu.make_async_copy(source.at[at], target.at[at], sems.at[i]))
    return out


def begin(many):
    for copy in many:
        copy.start()


def finish(many):
    for copy in many:
        copy.wait()


def head_kernel(
    x_hbm, g_hbm, inner_hbm, outer_hbm, sent_hbm,
    x_buf, g_buf, inner_buf, outer_buf, sent_buf, inner_wide, outer_wide,
    weight_sems, x_sems, g_sems, first_sems, second_sems,
):
    tile = x_buf.shape[0] // TILES
    inner_copy = pltpu.make_async_copy(inner_hbm, inner_buf, weight_sems.at[0])
    outer_copy = pltpu.make_async_copy(outer_hbm, outer_buf, weight_sems.at[1])
    x_copies = copies(x_hbm, x_buf, x_sems, tile, 0)
    g_copies = copies(g_hbm, g_buf, g_sems, tile, 0)
    inner_copy.start()
    begin(x_copies[:1])
    outer_copy.start()
    begin(x_copies[1:])
    begin(g_copies)
    inner_copy.wait()
    fill_inner_t(inner_buf, inner_wide)
    outer_copy.wait()
    fill_outer(outer_buf, outer_wide)
    outs = []
    for part, wide, buf, loads, sems in (
        (0, inner_wide, x_buf, x_copies, first_sems),
        (1, outer_wide, g_buf, g_copies, second_sems),
    ):
        band = pl.ds(16 * part, 16)
        stores = copies(sent_buf.at[:, band, :], sent_hbm.at[:, band, :], sems, tile, 2)
        outs += stores
        for i in range(TILES):
            loads[i].wait()
            mid = dot(wide[...], buf[tile * i:tile * i + tile, :], 1, 1).astype(BF)
            sent_buf[:, 16 * part:16 * part + 16, tile * i:tile * i + tile] = mid.reshape(32, 16, tile)
            stores[i].start()
    finish(outs)


def middle_kernel(
    got_hbm, outer_hbm, inner_hbm, sent_hbm, hidden_hbm, grad_pre_hbm,
    got_buf, outer_buf, inner_buf, sent_buf, hidden_buf, grad_pre_buf, pre_ref, slope_ref,
    outer_wide, outer_wide_t, inner_wide, inner_wide_t,
    weight_sems, got_sems, sent_sems, hidden_sems, grad_pre_sems,
):
    tile = hidden_buf.shape[1] // TILES
    outer_copy = pltpu.make_async_copy(outer_hbm, outer_buf, weight_sems.at[0])
    inner_copy = pltpu.make_async_copy(inner_hbm, inner_buf, weight_sems.at[1])
    loads = copies(got_hbm, got_buf, got_sems, tile, 2)
    sent_stores = copies(sent_buf, sent_hbm, sent_sems, tile, 2)
    hidden_stores = copies(hidden_buf, hidden_hbm, hidden_sems, tile, 1)
    grad_pre_stores = copies(grad_pre_buf, grad_pre_hbm, grad_pre_sems, tile, 1)
    outer_copy.start()
    inner_copy.start()
    begin(loads)
    outer_copy.wait()
    fill_outer_t(outer_buf, outer_wide_t)
    fill_outer(outer_buf, outer_wide)
    inner_copy.wait()
    fill_inner_t(inner_buf, inner_wide_t)
    fill_inner(inner_buf, inner_wide)
    for i in range(TILES):
        lanes = slice(tile * i, tile * i + tile)
        loads[i].wait()
        pre_ref[...] = dot(outer_wide_t[...], rows(got_buf[:, 0:16, lanes]), 1, 0)
        for top in range(0, 512, ROWS):
            band = slice(top, top + ROWS)
            pre = pre_ref[band, :]
            square = pre * pre
            bent = jnp.tanh(pre * (GELU_SCALE + (GELU_SCALE * GELU_CUBE) * square))
            half = 0.5 + 0.5 * bent
            hidden_buf[band, lanes] = (pre * half).astype(BF)
            rise = 0.5 * GELU_SCALE + (1.5 * GELU_SCALE * GELU_CUBE) * square
            slope_ref[band, :] = half + pre * (1.0 - bent * bent) * rise
        hidden_stores[i].start()
        mid = dot(inner_wide_t[...], hidden_buf[:, lanes], 1, 0).astype(BF)
        sent_buf[:, 0:16, lanes] = mid.reshape(32, 16, tile)
        grad_hidden = dot(inner_wide[...], rows(got_buf[:, 16:32, lanes]), 1, 0)
        grad_pre_buf[:, lanes] = (grad_hidden * slope_ref[...]).astype(BF)
        grad_pre_stores[i].start()
        grad_perm = dot(outer_wide[...], grad_pre_buf[:, lanes], 1, 0).astype(BF)
        sent_buf[:, 16:32, lanes] = grad_perm.reshape(32, 16, tile)
        sent_stores[i].start()
    finish(hidden_stores)
    finish(grad_pre_stores)
    finish(sent_stores)


def picked(total_ref, by_j):
    row = lax.broadcasted_iota(jnp.int32, (512, 128), 0)
    mine = (row // 4) % 4 if by_j else row % 4
    value = total_ref[:, 0:128]
    for block in range(1, 4):
        value = jnp.where(mine == block, total_ref[:, 128 * block:128 * block + 128], value)
    return value


def write_outer(total_ref, picked_ref, block_ref, out_ref, at):
    picked_ref[...] = picked(total_ref, True)
    for j in range(4):
        for b in range(4):
            block_ref[pl.ds(b, 32, stride=4), :] = picked_ref[pl.ds(4 * j + b, 32, stride=16), :]
        for rank in range(8):
            out_ref[rank, at + 16 * j:at + 16 * j + 16, :] = block_ref[16 * rank:16 * rank + 16, :].astype(out_ref.dtype)


def write_inner(total_ref, picked_ref, out_ref, at):
    picked_ref[...] = picked(total_ref, False)
    for b in range(4):
        block = picked_ref[pl.ds(b, 128, stride=4), :].T.astype(out_ref.dtype)
        for rank in range(8):
            out_ref[rank, at + 16 * b:at + 16 * b + 16, :] = block[16 * rank:16 * rank + 16, :]


def add(total_ref, value, start):
    if start:
        total_ref[...] = value
    else:
        total_ref[...] += value


def grads_kernel(
    dims, outer_part, inner_part, got_hbm, outer_other_hbm, inner_other_hbm, out_ref,
    got_buf, outer_other, inner_other, outer_total, inner_total, picked_ref, block_ref,
    got_sems, outer_sems, inner_sems,
):
    tile = got_buf.shape[2] // TILES
    loads = copies(got_hbm, got_buf, got_sems, tile, 2)
    outer_loads = copies(outer_other_hbm, outer_other, outer_sems, tile, dims[1])
    inner_loads = copies(inner_other_hbm, inner_other, inner_sems, tile, dims[1])
    for i in range(TILES):
        begin([loads[i], outer_loads[i], inner_loads[i]])
    for i in range(TILES):
        lanes = slice(tile * i, tile * i + tile)
        finish([loads[i], outer_loads[i], inner_loads[i]])
        at = (slice(None), lanes) if dims[1] else (lanes, slice(None))
        outer_rows = rows(got_buf[:, 16 * outer_part:16 * outer_part + 16, lanes])
        inner_rows = rows(got_buf[:, 16 * inner_part:16 * inner_part + 16, lanes])
        add(outer_total, dot(outer_rows, outer_other[at], *dims), i == 0)
        add(inner_total, dot(inner_rows, inner_other[at], *dims), i == 0)
    write_outer(outer_total, picked_ref, block_ref, out_ref, 0)
    write_inner(inner_total, picked_ref, out_ref, 64)


def tail_kernel(got_ref, outer_ref, inner_ref, output_ref, input_grad_ref, outer_wide, inner_wide):
    @pl.when(pl.program_id(0) == 0)
    def _():
        fill_outer(outer_ref, outer_wide)
        fill_inner_t(inner_ref, inner_wide)

    output_ref[...] = dot(rows(got_ref[:, 0:16, :]), outer_wide[...], 0, 0).astype(BF)
    input_grad_ref[...] = dot(rows(got_ref[:, 16:32, :]), inner_wide[...], 0, 0).astype(BF)


def call(kernel, name, args, outs, specs, out_specs, scratch, flops, grid=()):
    moved = sum(a.size * a.dtype.itemsize for a in args)
    moved += sum(o.size * o.dtype.itemsize for o in outs)
    return pl.pallas_call(
        kernel,
        grid=grid,
        in_specs=specs,
        out_specs=out_specs,
        out_shape=outs,
        scratch_shapes=scratch,
        name=name,
        cost_estimate=pl.CostEstimate(flops=flops, bytes_accessed=moved, transcendentals=0),
        compiler_params=pltpu.CompilerParams(vmem_limit_bytes=60 * 1024 * 1024),
    )(*args)


def body(tokens, inner_one, outer_one, inner_two, outer_two, cotangent):
    tok = tokens.shape[0]
    one = 2 * tok * 512 * 512
    shape = jax.ShapeDtypeStruct
    hbm = pl.BlockSpec(memory_space=pl.ANY)
    message = shape((32, 32, tok), BF)
    feature = shape((512, tok), BF)
    token_out = shape((tok, 512), BF)
    weight = pltpu.VMEM((4, 128, 128), BF)
    by_token = pltpu.VMEM((tok, 512), BF)
    by_feature = pltpu.VMEM((512, tok), BF)
    by_message = pltpu.VMEM((32, 32, tok), BF)
    wide = pltpu.VMEM((512, 512), BF)
    total = pltpu.VMEM((512, 512), F32)
    tile_f32 = pltpu.VMEM((512, tok // TILES), F32)
    pair = pltpu.SemaphoreType.DMA((2,))
    sems = pltpu.SemaphoreType.DMA((TILES,))

    def exchange(value, axis):
        return lax.all_to_all(value, axis, split_axis=0, concat_axis=0, tiled=True)

    def grads(got, outer_part, outer_other, inner_part, inner_other, dims, kind, name):
        buf = by_feature if dims[1] else by_token
        return call(
            lambda *refs: grads_kernel(dims, outer_part, inner_part, *refs), name,
            (got, outer_other, inner_other), [shape((8, 128, 128), kind)], [hbm] * 3,
            [pl.BlockSpec(memory_space=pltpu.VMEM)],
            [by_message, buf, buf, total, total, pltpu.VMEM((512, 128), F32), pltpu.VMEM((128, 128), F32), sems, sems, sems],
            2 * one,
        )[0]

    sent = call(
        head_kernel, "head", (tokens, cotangent, inner_one, outer_two), [message], [hbm] * 4, [hbm],
        [by_token, by_token, weight, weight, by_message, wide, wide, pair, sems, sems, sems, sems], 2 * one,
    )[0]
    got = exchange(sent, "mp")
    sent_two, hidden, grad_pre = call(
        middle_kernel, "middle", (got, outer_one, inner_two), [message, feature, feature], [hbm] * 3, [hbm] * 3,
        [by_message, weight, weight, by_message, by_feature, by_feature, tile_f32, tile_f32,
         wide, wide, wide, wide, pair, sems, sems, sems, sems], 4 * one,
    )
    got_two = exchange(sent_two, "mp")
    early = grads(got, 0, grad_pre, 1, hidden, (1, 1), F32, "early_grads")
    early = lax.psum_scatter(early, "dp", scatter_dimension=0, tiled=True)
    late = exchange(grads(got_two, 0, cotangent, 1, tokens, (1, 0), BF, "late_grads"), "dp")
    step = tok // 2
    weights = pl.BlockSpec((4, 128, 128), lambda i: (0, 0, 0))
    tokens_at = pl.BlockSpec((step, 512), lambda i: (i, 0))
    output, input_grad = call(
        tail_kernel, "tail", (got_two, outer_two, inner_one), [token_out, token_out],
        [pl.BlockSpec((32, 32, step), lambda i: (0, 0, i)), weights, weights], [tokens_at, tokens_at],
        [wide, wide], 2 * one, (2,),
    )
    return (
        output,
        input_grad,
        jnp.sum(late[:, 64:], axis=0, dtype=F32).reshape(4, 16, 128),
        early[0, :64].reshape(4, 16, 128),
        early[0, 64:].reshape(4, 16, 128),
        jnp.sum(late[:, :64], axis=0, dtype=F32).reshape(4, 16, 128),
    )


def solution(mesh):
    placed = (
        P("dp", "mp"),
        P("mp", None, None),
        P("mp", None, None),
        P("mp", None, None),
        P("mp", None, None),
        P("dp", "mp"),
    )
    return jax.shard_map(
        body,
        mesh=mesh,
        in_specs=placed,
        out_specs=(
            P("dp", "mp"),
            P("dp", "mp"),
            P("mp", "dp", None),
            P("mp", "dp", None),
            P("mp", "dp", None),
            P("mp", "dp", None),
        ),
        check_vma=False,
    )
```

```python
import jax
import jax.numpy as jnp
from jax import lax
from jax.experimental import pallas as pl
from jax.experimental.pallas import tpu as pltpu
from jax.sharding import PartitionSpec as P

BF = jnp.bfloat16
F32 = jnp.float32
GELU_SCALE = 0.7978845608028654
GELU_CUBE = 0.044715
TILES = 4
ROWS = 64


def dot(left, right, left_dim, right_dim):
    return lax.dot_general(
        left, right, (((left_dim,), (right_dim,)), ((), ())), preferred_element_type=F32
    )


def inner_spread(block, wide, rows_wide):
    shape = (wide, 128) if rows_wide else (128, wide)
    row = lax.broadcasted_iota(jnp.int32, shape, 0)
    col = lax.broadcasted_iota(jnp.int32, shape, 1)
    hit = (row == 4 * col + block) if rows_wide else (col == 4 * row + block)
    return hit.astype(F32).astype(BF)


def outer_spread(block):
    row = lax.broadcasted_iota(jnp.int32, (512, 128), 0)
    col = lax.broadcasted_iota(jnp.int32, (512, 128), 1)
    hit = row == 16 * (col // 4) + 4 * block + col % 4
    return hit.astype(F32).astype(BF)


def fill_inner_t(weight_ref, wide_ref):
    for block in range(4):
        wide_ref[:, 128 * block:128 * block + 128] = dot(
            inner_spread(block, 512, True), weight_ref[block], 1, 1
        ).astype(BF)


def fill_inner(weight_ref, wide_ref):
    for block in range(4):
        wide_ref[128 * block:128 * block + 128, :] = dot(
            weight_ref[block], inner_spread(block, 512, False), 1, 0
        ).astype(BF)


def fill_outer(weight_ref, wide_ref):
    for block in range(4):
        wide_ref[:, 128 * block:128 * block + 128] = dot(
            outer_spread(block), weight_ref[block], 1, 0
        ).astype(BF)


def fill_outer_t(weight_ref, wide_ref):
    for block in range(4):
        wide_ref[128 * block:128 * block + 128, :] = dot(
            weight_ref[block], outer_spread(block), 0, 1
        ).astype(BF)


def rows(value):
    return value.reshape(512, value.shape[-1])


def copies(source, target, sems, tile, axis):
    out = []
    for i in range(TILES):
        at = (slice(None),) * axis + (pl.ds(tile * i, tile),)
        out.append(pltpu.make_async_copy(source.at[at], target.at[at], sems.at[i]))
    return out


def begin(many):
    for copy in many:
        copy.start()


def finish(many):
    for copy in many:
        copy.wait()


def head_kernel(
    x_hbm, g_hbm, inner_hbm, outer_hbm, sent_hbm,
    x_buf, g_buf, inner_buf, outer_buf, sent_buf, inner_wide, outer_wide,
    weight_sems, x_sems, g_sems, first_sems, second_sems,
):
    tile = x_buf.shape[0] // TILES
    inner_copy = pltpu.make_async_copy(inner_hbm, inner_buf, weight_sems.at[0])
    outer_copy = pltpu.make_async_copy(outer_hbm, outer_buf, weight_sems.at[1])
    x_copies = copies(x_hbm, x_buf, x_sems, tile, 0)
    g_copies = copies(g_hbm, g_buf, g_sems, tile, 0)
    inner_copy.start()
    begin(x_copies[:1])
    outer_copy.start()
    begin(x_copies[1:])
    begin(g_copies)
    inner_copy.wait()
    fill_inner_t(inner_buf, inner_wide)
    outer_copy.wait()
    fill_outer(outer_buf, outer_wide)
    outs = []
    for part, wide, buf, loads, sems in (
        (0, inner_wide, x_buf, x_copies, first_sems),
        (1, outer_wide, g_buf, g_copies, second_sems),
    ):
        band = pl.ds(16 * part, 16)
        stores = copies(sent_buf.at[:, band, :], sent_hbm.at[:, band, :], sems, tile, 2)
        outs += stores
        for i in range(TILES):
            loads[i].wait()
            mid = dot(wide[...], buf[tile * i:tile * i + tile, :], 1, 1).astype(BF)
            sent_buf[:, 16 * part:16 * part + 16, tile * i:tile * i + tile] = mid.reshape(32, 16, tile)
            stores[i].start()
    finish(outs)


def middle_kernel(
    got_hbm, outer_hbm, inner_hbm, sent_hbm, hidden_hbm, grad_pre_hbm,
    got_buf, outer_buf, inner_buf, sent_buf, hidden_buf, grad_pre_buf, pre_ref, slope_ref,
    outer_wide, outer_wide_t, inner_wide, inner_wide_t,
    weight_sems, got_sems, sent_sems, hidden_sems, grad_pre_sems,
):
    tile = hidden_buf.shape[1] // TILES
    outer_copy = pltpu.make_async_copy(outer_hbm, outer_buf, weight_sems.at[0])
    inner_copy = pltpu.make_async_copy(inner_hbm, inner_buf, weight_sems.at[1])
    loads = copies(got_hbm, got_buf, got_sems, tile, 2)
    sent_stores = copies(sent_buf, sent_hbm, sent_sems, tile, 2)
    hidden_stores = copies(hidden_buf, hidden_hbm, hidden_sems, tile, 1)
    grad_pre_stores = copies(grad_pre_buf, grad_pre_hbm, grad_pre_sems, tile, 1)
    outer_copy.start()
    inner_copy.start()
    begin(loads)
    outer_copy.wait()
    fill_outer_t(outer_buf, outer_wide_t)
    fill_outer(outer_buf, outer_wide)
    inner_copy.wait()
    fill_inner_t(inner_buf, inner_wide_t)
    fill_inner(inner_buf, inner_wide)
    for i in range(TILES):
        lanes = slice(tile * i, tile * i + tile)
        loads[i].wait()
        pre_ref[...] = dot(outer_wide_t[...], rows(got_buf[:, 0:16, lanes]), 1, 0)
        for top in range(0, 512, ROWS):
            band = slice(top, top + ROWS)
            pre = pre_ref[band, :]
            square = pre * pre
            bent = jnp.tanh(pre * (GELU_SCALE + (GELU_SCALE * GELU_CUBE) * square))
            half = 0.5 + 0.5 * bent
            hidden_buf[band, lanes] = (pre * half).astype(BF)
            rise = 0.5 * GELU_SCALE + (1.5 * GELU_SCALE * GELU_CUBE) * square
            slope_ref[band, :] = half + pre * (1.0 - bent * bent) * rise
        hidden_stores[i].start()
        mid = dot(inner_wide_t[...], hidden_buf[:, lanes], 1, 0).astype(BF)
        sent_buf[:, 0:16, lanes] = mid.reshape(32, 16, tile)
        grad_hidden = dot(inner_wide[...], rows(got_buf[:, 16:32, lanes]), 1, 0)
        grad_pre_buf[:, lanes] = (grad_hidden * slope_ref[...]).astype(BF)
        grad_pre_stores[i].start()
        grad_perm = dot(outer_wide[...], grad_pre_buf[:, lanes], 1, 0).astype(BF)
        sent_buf[:, 16:32, lanes] = grad_perm.reshape(32, 16, tile)
        sent_stores[i].start()
    finish(hidden_stores)
    finish(grad_pre_stores)
    finish(sent_stores)


def picked(total_ref, by_j):
    row = lax.broadcasted_iota(jnp.int32, (512, 128), 0)
    mine = (row // 4) % 4 if by_j else row % 4
    value = total_ref[:, 0:128]
    for block in range(1, 4):
        value = jnp.where(mine == block, total_ref[:, 128 * block:128 * block + 128], value)
    return value


def spread_out(block_ref, slots, at):
    for rank, out_ref in slots:
        first_row = 16 * rank if isinstance(rank, int) else pl.multiple_of(16 * rank, 16)
        out_ref[at:at + 16, :] = block_ref[pl.ds(first_row, 16), :].astype(out_ref.dtype)


def write_outer(total_ref, picked_ref, block_ref, slots, at):
    picked_ref[...] = picked(total_ref, True)
    for j in range(4):
        for b in range(4):
            block_ref[pl.ds(b, 32, stride=4), :] = picked_ref[pl.ds(4 * j + b, 32, stride=16), :]
        spread_out(block_ref, slots, at + 16 * j)


def write_inner(total_ref, picked_ref, block_ref, slots, at):
    picked_ref[...] = picked(total_ref, False)
    for b in range(4):
        block_ref[...] = picked_ref[pl.ds(b, 128, stride=4), :].T
        spread_out(block_ref, slots, at + 16 * b)


def add(total_ref, value, start):
    if start:
        total_ref[...] = value
    else:
        total_ref[...] += value


def grads_kernel(
    dims, outer_part, inner_part, got_hbm, outer_other_hbm, inner_other_hbm, mine_ref, *refs
):
    if len(refs) == 11:
        slots = [(rank, refs[0].at[rank]) for rank in range(8)]
    else:
        order = [(0, 0), (1, 0), (2, 0), (2, 128), (3, 0), (3, 128), (3, 256), (3, 384)]
        slots = [(mine_ref[0] ^ i, refs[out].at[pl.ds(row, 128), :]) for i, (out, row) in enumerate(order)]
    got_buf, outer_other, inner_other, outer_total, inner_total = refs[-10:-5]
    picked_ref, block_ref, got_sems, outer_sems, inner_sems = refs[-5:]
    tile = got_buf.shape[2] // TILES
    loads = copies(got_hbm, got_buf, got_sems, tile, 2)
    outer_loads = copies(outer_other_hbm, outer_other, outer_sems, tile, dims[1])
    inner_loads = copies(inner_other_hbm, inner_other, inner_sems, tile, dims[1])
    for i in range(TILES):
        begin([loads[i], outer_loads[i], inner_loads[i]])
    for i in range(TILES):
        lanes = slice(tile * i, tile * i + tile)
        finish([loads[i], outer_loads[i], inner_loads[i]])
        at = (slice(None), lanes) if dims[1] else (lanes, slice(None))
        outer_rows = rows(got_buf[:, 16 * outer_part:16 * outer_part + 16, lanes])
        inner_rows = rows(got_buf[:, 16 * inner_part:16 * inner_part + 16, lanes])
        add(outer_total, dot(outer_rows, outer_other[at], *dims), i == 0)
        add(inner_total, dot(inner_rows, inner_other[at], *dims), i == 0)
    write_outer(outer_total, picked_ref, block_ref, slots, 0)
    write_inner(inner_total, picked_ref, block_ref, slots, 64)


def tail_kernel(got_ref, outer_ref, inner_ref, output_ref, input_grad_ref, outer_wide, inner_wide):
    @pl.when(pl.program_id(0) == 0)
    def _():
        fill_outer(outer_ref, outer_wide)
        fill_inner_t(inner_ref, inner_wide)

    output_ref[...] = dot(rows(got_ref[:, 0:16, :]), outer_wide[...], 0, 0).astype(BF)
    input_grad_ref[...] = dot(rows(got_ref[:, 16:32, :]), inner_wide[...], 0, 0).astype(BF)


def call(kernel, name, args, outs, specs, out_specs, scratch, flops, grid=()):
    moved = sum(a.size * a.dtype.itemsize for a in args)
    moved += sum(o.size * o.dtype.itemsize for o in outs)
    return pl.pallas_call(
        kernel,
        grid=grid,
        in_specs=specs,
        out_specs=out_specs,
        out_shape=outs,
        scratch_shapes=scratch,
        name=name,
        cost_estimate=pl.CostEstimate(flops=flops, bytes_accessed=moved, transcendentals=0),
        compiler_params=pltpu.CompilerParams(vmem_limit_bytes=60 * 1024 * 1024),
    )(*args)


def body(tokens, inner_one, outer_one, inner_two, outer_two, cotangent):
    tok = tokens.shape[0]
    one = 2 * tok * 512 * 512
    mine = lax.axis_index("dp").astype(jnp.int32).reshape(1)
    shape = jax.ShapeDtypeStruct
    hbm = pl.BlockSpec(memory_space=pl.ANY)
    message = shape((32, 32, tok), BF)
    feature = shape((512, tok), BF)
    token_out = shape((tok, 512), BF)
    weight = pltpu.VMEM((4, 128, 128), BF)
    by_token = pltpu.VMEM((tok, 512), BF)
    by_feature = pltpu.VMEM((512, tok), BF)
    by_message = pltpu.VMEM((32, 32, tok), BF)
    wide = pltpu.VMEM((512, 512), BF)
    total = pltpu.VMEM((512, 512), F32)
    tile_f32 = pltpu.VMEM((512, tok // TILES), F32)
    pair = pltpu.SemaphoreType.DMA((2,))
    sems = pltpu.SemaphoreType.DMA((TILES,))

    def exchange(value, axis):
        return lax.all_to_all(value, axis, split_axis=0, concat_axis=0, tiled=True)

    def across(value, flip):
        return lax.ppermute(value, "dp", [(rank, rank ^ flip) for rank in range(8)])

    def grads(got, outer_part, outer_other, inner_part, inner_other, dims, outs, name):
        buf = by_feature if dims[1] else by_token
        return call(
            lambda *refs: grads_kernel(dims, outer_part, inner_part, *refs), name,
            (got, outer_other, inner_other, mine), outs,
            [hbm] * 3 + [pl.BlockSpec(memory_space=pltpu.SMEM)],
            [pl.BlockSpec(memory_space=pltpu.VMEM)] * len(outs),
            [by_message, buf, buf, total, total, pltpu.VMEM((512, 128), F32), pltpu.VMEM((128, 128), F32), sems, sems, sems],
            2 * one,
        )

    sent = call(
        head_kernel, "head", (tokens, cotangent, inner_one, outer_two), [message], [hbm] * 4, [hbm],
        [by_token, by_token, weight, weight, by_message, wide, wide, pair, sems, sems, sems, sems], 2 * one,
    )[0]
    got = exchange(sent, "mp")
    sent_two, hidden, grad_pre = call(
        middle_kernel, "middle", (got, outer_one, inner_two), [message, feature, feature], [hbm] * 3, [hbm] * 3,
        [by_message, weight, weight, by_message, by_feature, by_feature, tile_f32, tile_f32,
         wide, wide, wide, wide, pair, sems, sems, sems, sems], 4 * one,
    )
    got_two = exchange(sent_two, "mp")
    own, near, middle, far = grads(
        got, 0, grad_pre, 1, hidden, (1, 1), [shape((128 * n, 128), F32) for n in (1, 1, 2, 4)], "early_grads"
    )
    halves = across(far, 4)
    quarters = across(middle + halves[256:], 2)
    eighth = across(near + halves[128:256] + quarters[128:], 1)
    late = grads(got_two, 0, cotangent, 1, tokens, (1, 0), [shape((8, 128, 128), BF)], "late_grads")[0]
    late = exchange(late, "dp")
    step = tok // 2
    weights = pl.BlockSpec((4, 128, 128), lambda i: (0, 0, 0))
    tokens_at = pl.BlockSpec((step, 512), lambda i: (i, 0))
    output, input_grad = call(
        tail_kernel, "tail", (got_two, outer_two, inner_one), [token_out, token_out],
        [pl.BlockSpec((32, 32, step), lambda i: (0, 0, i)), weights, weights], [tokens_at, tokens_at],
        [wide, wide], 2 * one, (2,),
    )
    return (
        output,
        input_grad,
        jnp.sum(late[:, 64:], axis=0, dtype=F32).reshape(4, 16, 128),
        (own[:64] + halves[:64] + quarters[:64] + eighth[:64]).reshape(4, 16, 128),
        (own[64:] + halves[64:128] + quarters[64:128] + eighth[64:]).reshape(4, 16, 128),
        jnp.sum(late[:, :64], axis=0, dtype=F32).reshape(4, 16, 128),
    )


def solution(mesh):
    placed = (
        P("dp", "mp"),
        P("mp", None, None),
        P("mp", None, None),
        P("mp", None, None),
        P("mp", None, None),
        P("dp", "mp"),
    )
    return jax.shard_map(
        body,
        mesh=mesh,
        in_specs=placed,
        out_specs=(
            P("dp", "mp"),
            P("dp", "mp"),
            P("mp", "dp", None),
            P("mp", "dp", None),
            P("mp", "dp", None),
            P("mp", "dp", None),
        ),
        check_vma=False,
    )
```

```python
import jax
import jax.numpy as jnp
from jax import lax
from jax.experimental import pallas as pl
from jax.experimental.pallas import tpu as pltpu
from jax.sharding import PartitionSpec as P

BF = jnp.bfloat16
F32 = jnp.float32
GELU_SCALE = 0.7978845608028654
GELU_CUBE = 0.044715
TILES = 2
LATE_TILES = 4
ROWS = 64


def dot(left, right, left_dim, right_dim):
    return lax.dot_general(
        left, right, (((left_dim,), (right_dim,)), ((), ())), preferred_element_type=F32
    )


def inner_spread(block, wide, rows_wide):
    shape = (wide, 128) if rows_wide else (128, wide)
    row = lax.broadcasted_iota(jnp.int32, shape, 0)
    col = lax.broadcasted_iota(jnp.int32, shape, 1)
    hit = (row == 4 * col + block) if rows_wide else (col == 4 * row + block)
    return hit.astype(F32).astype(BF)


def outer_spread(block):
    row = lax.broadcasted_iota(jnp.int32, (512, 128), 0)
    col = lax.broadcasted_iota(jnp.int32, (512, 128), 1)
    hit = row == 16 * (col // 4) + 4 * block + col % 4
    return hit.astype(F32).astype(BF)


def fill_inner_t(weight_ref, wide_ref):
    for block in range(4):
        wide_ref[:, 128 * block:128 * block + 128] = dot(
            inner_spread(block, 512, True), weight_ref[block], 1, 1
        ).astype(BF)


def fill_inner(weight_ref, wide_ref):
    for block in range(4):
        wide_ref[128 * block:128 * block + 128, :] = dot(
            weight_ref[block], inner_spread(block, 512, False), 1, 0
        ).astype(BF)


def fill_outer(weight_ref, wide_ref):
    for block in range(4):
        wide_ref[:, 128 * block:128 * block + 128] = dot(
            outer_spread(block), weight_ref[block], 1, 0
        ).astype(BF)


def fill_outer_t(weight_ref, wide_ref):
    for block in range(4):
        wide_ref[128 * block:128 * block + 128, :] = dot(
            weight_ref[block], outer_spread(block), 0, 1
        ).astype(BF)


def rows(value):
    return value.reshape(512, value.shape[-1])


def copies(source, target, sems, tile, axis):
    out = []
    for i in range(source.shape[axis] // tile):
        at = (slice(None),) * axis + (pl.ds(tile * i, tile),)
        out.append(pltpu.make_async_copy(source.at[at], target.at[at], sems.at[i]))
    return out


def begin(many):
    for copy in many:
        copy.start()


def finish(many):
    for copy in many:
        copy.wait()


def load(pairs, sems):
    out = [pltpu.make_async_copy(source, target, sems.at[i]) for i, (source, target) in enumerate(pairs)]
    begin(out)
    return out


def head_kernel(
    x_hbm, g_hbm, inner_hbm, outer_hbm, sent_ref,
    x_buf, g_buf, inner_buf, outer_buf, inner_wide, outer_wide, weight_sems, x_sems, g_sems,
):
    tile = x_buf.shape[0] // TILES
    weights = load([(inner_hbm, inner_buf), (outer_hbm, outer_buf)], weight_sems)
    x_copies = copies(x_hbm, x_buf, x_sems, tile, 0)
    g_copies = copies(g_hbm, g_buf, g_sems, tile, 0)
    begin(x_copies)
    begin(g_copies)
    finish(weights)
    fill_inner_t(inner_buf, inner_wide)
    fill_outer(outer_buf, outer_wide)
    for part, wide, buf, arriving in ((0, inner_wide, x_buf, x_copies), (1, outer_wide, g_buf, g_copies)):
        for i in range(TILES):
            arriving[i].wait()
            mid = dot(wide[...], buf[tile * i:tile * i + tile, :], 1, 1).astype(BF)
            sent_ref[:, 16 * part:16 * part + 16, tile * i:tile * i + tile] = mid.reshape(32, 16, tile)


def activate(pre_ref, slope_ref, hidden_ref):
    for top in range(0, 512, ROWS):
        band = slice(top, top + ROWS)
        pre = pre_ref[band, :]
        square = pre * pre
        bent = jnp.tanh(pre * (GELU_SCALE + (GELU_SCALE * GELU_CUBE) * square))
        half = 0.5 + 0.5 * bent
        hidden_ref[band, :] = (pre * half).astype(BF)
        rise = 0.5 * GELU_SCALE + (1.5 * GELU_SCALE * GELU_CUBE) * square
        slope_ref[band, :] = half + pre * (1.0 - bent * bent) * rise


def middle_kernel(
    got_ref, outer_hbm, inner_hbm, sent_hbm, kept_hbm,
    outer_buf, inner_buf, sent_buf, pre_ref, slope_ref, hidden_ref, grad_pre_ref,
    outer_wide, outer_wide_t, inner_wide, inner_wide_t, weight_sems, sent_sems, kept_sem,
):
    tile = got_ref.shape[2] // TILES
    outer_copy, inner_copy = load([(outer_hbm, outer_buf), (inner_hbm, inner_buf)], weight_sems)
    kept_copy = pltpu.make_async_copy(got_ref, kept_hbm, kept_sem)
    kept_copy.start()
    sent_stores = copies(sent_buf, sent_hbm, sent_sems, tile, 2)
    outer_copy.wait()
    fill_outer_t(outer_buf, outer_wide_t)
    fill_outer(outer_buf, outer_wide)
    inner_copy.wait()
    fill_inner_t(inner_buf, inner_wide_t)
    fill_inner(inner_buf, inner_wide)
    for i in range(TILES):
        lanes = slice(tile * i, tile * i + tile)
        pre_ref[...] = dot(outer_wide_t[...], rows(got_ref[:, 0:16, lanes]), 1, 0)
        activate(pre_ref, slope_ref, hidden_ref)
        mid = dot(inner_wide_t[...], hidden_ref[...], 1, 0).astype(BF)
        sent_buf[:, 0:16, lanes] = mid.reshape(32, 16, tile)
        grad_hidden = dot(inner_wide[...], rows(got_ref[:, 16:32, lanes]), 1, 0)
        grad_pre_ref[...] = (grad_hidden * slope_ref[...]).astype(BF)
        grad_perm = dot(outer_wide[...], grad_pre_ref[...], 1, 0).astype(BF)
        sent_buf[:, 16:32, lanes] = grad_perm.reshape(32, 16, tile)
        sent_stores[i].start()
    finish(sent_stores)
    kept_copy.wait()


def picked(total_ref, by_j):
    row = lax.broadcasted_iota(jnp.int32, (512, 128), 0)
    mine = (row // 4) % 4 if by_j else row % 4
    value = total_ref[:, 0:128]
    for block in range(1, 4):
        value = jnp.where(mine == block, total_ref[:, 128 * block:128 * block + 128], value)
    return value


def spread_out(block_ref, slots, at):
    for rank, out_ref in slots:
        first_row = 16 * rank if isinstance(rank, int) else pl.multiple_of(16 * rank, 16)
        out_ref[at:at + 16, :] = block_ref[pl.ds(first_row, 16), :].astype(out_ref.dtype)


def write_outer(total_ref, picked_ref, block_ref, slots, at):
    picked_ref[...] = picked(total_ref, True)
    for j in range(4):
        for b in range(4):
            block_ref[pl.ds(b, 32, stride=4), :] = picked_ref[pl.ds(4 * j + b, 32, stride=16), :]
        spread_out(block_ref, slots, at + 16 * j)


def write_inner(total_ref, picked_ref, block_ref, slots, at):
    picked_ref[...] = picked(total_ref, False)
    for b in range(4):
        block_ref[...] = picked_ref[pl.ds(b, 128, stride=4), :].T
        spread_out(block_ref, slots, at + 16 * b)


def add(total_ref, value, start):
    if start:
        total_ref[...] = value
    else:
        total_ref[...] += value


def early_kernel(
    got_ref, outer_hbm, inner_hbm, mine_ref, own_ref, near_ref, middle_ref, far_ref,
    outer_buf, inner_buf, pre_ref, slope_ref, hidden_ref, grad_pre_ref, outer_wide_t, inner_wide,
    outer_total, inner_total, picked_ref, block_ref, weight_sems,
):
    tile = got_ref.shape[2] // TILES
    finish(load([(outer_hbm, outer_buf), (inner_hbm, inner_buf)], weight_sems))
    fill_outer_t(outer_buf, outer_wide_t)
    fill_inner(inner_buf, inner_wide)
    for i in range(TILES):
        lanes = slice(tile * i, tile * i + tile)
        first_perm = rows(got_ref[:, 0:16, lanes])
        grad_mid = rows(got_ref[:, 16:32, lanes])
        pre_ref[...] = dot(outer_wide_t[...], first_perm, 1, 0)
        activate(pre_ref, slope_ref, hidden_ref)
        grad_hidden = dot(inner_wide[...], grad_mid, 1, 0)
        grad_pre_ref[...] = (grad_hidden * slope_ref[...]).astype(BF)
        add(outer_total, dot(first_perm, grad_pre_ref[...], 1, 1), i == 0)
        add(inner_total, dot(grad_mid, hidden_ref[...], 1, 1), i == 0)
    slabs = [(own_ref, 0), (near_ref, 0), (middle_ref, 0), (middle_ref, 128)] + [(far_ref, 128 * i) for i in range(4)]
    slots = [(mine_ref[0] ^ i, ref.at[pl.ds(row, 128), :]) for i, (ref, row) in enumerate(slabs)]
    write_outer(outer_total, picked_ref, block_ref, slots, 0)
    write_inner(inner_total, picked_ref, block_ref, slots, 64)


def late_kernel(
    got_hbm, x_hbm, g_hbm, out_ref,
    got_buf, x_buf, g_buf, outer_total, inner_total, picked_ref, block_ref, second_sems, grad_sems, x_sems, g_sems,
):
    tile = x_buf.shape[0] // LATE_TILES
    slots = [(rank, out_ref.at[rank]) for rank in range(8)]
    g_copies = copies(g_hbm, g_buf, g_sems, tile, 0)
    x_copies = copies(x_hbm, x_buf, x_sems, tile, 0)
    second = copies(got_hbm.at[:, 0:16, :], got_buf.at[:, 0:16, :], second_sems, tile, 2)
    grad = copies(got_hbm.at[:, 16:32, :], got_buf.at[:, 16:32, :], grad_sems, tile, 2)
    for i in range(LATE_TILES):
        begin([second[i], g_copies[i]])
    for i in range(LATE_TILES):
        begin([grad[i], x_copies[i]])
    for i in range(LATE_TILES):
        lanes = slice(tile * i, tile * i + tile)
        finish([second[i], g_copies[i]])
        add(outer_total, dot(rows(got_buf[:, 0:16, lanes]), g_buf[lanes, :], 1, 0), i == 0)
    write_outer(outer_total, picked_ref, block_ref, slots, 0)
    for i in range(LATE_TILES):
        lanes = slice(tile * i, tile * i + tile)
        finish([grad[i], x_copies[i]])
        add(inner_total, dot(rows(got_buf[:, 16:32, lanes]), x_buf[lanes, :], 1, 0), i == 0)
    write_inner(inner_total, picked_ref, block_ref, slots, 64)


def tail_kernel(
    got_ref, outer_hbm, inner_hbm, output_hbm, input_grad_hbm,
    output_buf, input_grad_buf, outer_buf, inner_buf, outer_wide, inner_wide, weight_sems, output_sems, input_grad_sems,
):
    tile = output_buf.shape[0] // TILES
    finish(load([(outer_hbm, outer_buf), (inner_hbm, inner_buf)], weight_sems))
    fill_outer(outer_buf, outer_wide)
    fill_inner_t(inner_buf, inner_wide)
    stores = []
    for part, wide, buf, out, sems in (
        (0, outer_wide, output_buf, output_hbm, output_sems),
        (1, inner_wide, input_grad_buf, input_grad_hbm, input_grad_sems),
    ):
        leaving = copies(buf, out, sems, tile, 0)
        stores += leaving
        for i in range(TILES):
            lanes = slice(tile * i, tile * i + tile)
            message = rows(got_ref[:, 16 * part:16 * part + 16, lanes])
            buf[lanes, :] = dot(message, wide[...], 0, 0).astype(BF)
            leaving[i].start()
    finish(stores)


def call(kernel, name, args, outs, specs, out_specs, scratch, flops):
    moved = 2 * sum(a.size for a in args)
    return pl.pallas_call(
        kernel,
        in_specs=specs,
        out_specs=out_specs,
        out_shape=outs,
        scratch_shapes=scratch,
        name=name,
        cost_estimate=pl.CostEstimate(flops=flops, bytes_accessed=moved, transcendentals=0),
        compiler_params=pltpu.CompilerParams(vmem_limit_bytes=24 * 1024 * 1024),
    )(*args)


def body(tokens, inner_one, outer_one, inner_two, outer_two, cotangent):
    tok = tokens.shape[0]
    one = 2 * tok * 512 * 512
    mine = lax.axis_index("dp").astype(jnp.int32).reshape(1)
    tokens, cotangent, inner_one, outer_one, inner_two, outer_two = (
        pltpu.with_memory_space_constraint(value, pltpu.HBM)
        for value in (tokens, cotangent, inner_one, outer_one, inner_two, outer_two)
    )
    shape = jax.ShapeDtypeStruct
    hbm = pl.BlockSpec(memory_space=pltpu.HBM)
    vmem = pl.BlockSpec(memory_space=pltpu.VMEM)
    smem = pl.BlockSpec(memory_space=pltpu.SMEM)
    weight = pltpu.VMEM((4, 128, 128), BF)
    by_token = pltpu.VMEM((tok, 512), BF)
    by_message = pltpu.VMEM((32, 32, tok), BF)
    wide = pltpu.VMEM((512, 512), BF)
    total = pltpu.VMEM((512, 512), F32)
    picked_part = pltpu.VMEM((512, 128), F32)
    block = pltpu.VMEM((128, 128), F32)
    tile_f32 = pltpu.VMEM((512, tok // TILES), F32)
    tile_bf = pltpu.VMEM((512, tok // TILES), BF)
    pair = pltpu.SemaphoreType.DMA((2,))
    sems = pltpu.SemaphoreType.DMA((TILES,))
    late_sems = pltpu.SemaphoreType.DMA((LATE_TILES,))

    def exchange(value, axis):
        return lax.all_to_all(value, axis, split_axis=0, concat_axis=0, tiled=True)

    def across(value, flip):
        return lax.ppermute(value, "dp", [(rank, rank ^ flip) for rank in range(8)])

    sent = call(
        head_kernel, "head", (tokens, cotangent, inner_one, outer_two), [by_message], [hbm] * 4, [vmem],
        [by_token, by_token, weight, weight, wide, wide, pair, sems, sems], 2 * one,
    )[0]
    got = exchange(sent, "mp")
    sent_two, kept = call(
        middle_kernel, "middle", (got, outer_one, inner_two), [pltpu.HBM((32, 32, tok), BF)] * 2, [vmem, hbm, hbm], [hbm] * 2,
        [weight, weight, by_message, tile_f32, tile_f32, tile_bf, tile_bf, wide, wide, wide, wide, pair, sems, pltpu.SemaphoreType.DMA], 4 * one,
    )
    got_two = exchange(sent_two, "mp")
    own, near, middle, far = call(
        early_kernel, "early_grads", (kept, outer_one, inner_two, mine),
        [shape((128 * n, 128), F32) for n in (1, 1, 2, 4)], [vmem, hbm, hbm, smem], [vmem] * 4,
        [weight, weight, tile_f32, tile_f32, tile_bf, tile_bf, wide, wide, total, total, picked_part, block, pair], 4 * one,
    )
    halves = across(far, 4)
    quarters = across(middle + halves[256:], 2)
    eighth = across(near + halves[128:256] + quarters[128:], 1)
    got_two = pltpu.with_memory_space_constraint(got_two, pltpu.HBM)
    late = call(
        late_kernel, "late_grads", (got_two, tokens, cotangent), [shape((8, 128, 128), BF)], [hbm] * 3, [vmem],
        [by_message, by_token, by_token, total, total, picked_part, block] + [late_sems] * 4, 2 * one,
    )[0]
    late = exchange(late, "dp")
    output, input_grad = call(
        tail_kernel, "tail", (got_two, outer_two, inner_one), [pltpu.HBM((tok, 512), BF)] * 2, [vmem, hbm, hbm], [hbm] * 2,
        [by_token, by_token, weight, weight, wide, wide, pair, sems, sems], 2 * one,
    )
    return (
        output,
        input_grad,
        jnp.sum(late[:, 64:], axis=0, dtype=F32).reshape(4, 16, 128),
        (own[:64] + halves[:64] + quarters[:64] + eighth[:64]).reshape(4, 16, 128),
        (own[64:] + halves[64:128] + quarters[64:128] + eighth[64:]).reshape(4, 16, 128),
        jnp.sum(late[:, :64], axis=0, dtype=F32).reshape(4, 16, 128),
    )


def solution(mesh):
    placed = (
        P("dp", "mp"),
        P("mp", None, None),
        P("mp", None, None),
        P("mp", None, None),
        P("mp", None, None),
        P("dp", "mp"),
    )
    return jax.shard_map(
        body,
        mesh=mesh,
        in_specs=placed,
        out_specs=(
            P("dp", "mp"),
            P("dp", "mp"),
            P("mp", "dp", None),
            P("mp", "dp", None),
            P("mp", "dp", None),
            P("mp", "dp", None),
        ),
        check_vma=False,
    )
```

```python
import jax
import jax.numpy as jnp
from jax import lax
from jax.experimental import pallas as pl
from jax.experimental.pallas import tpu as pltpu
from jax.sharding import PartitionSpec as P

BF = jnp.bfloat16
F32 = jnp.float32
GELU_SCALE = 0.7978845608028654
GELU_CUBE = 0.044715
HEAD_TILES = 1
TILES = 4
LATE_TILES = 4
ROWS = 64

PEERS = [8 * y + 2 * x + core for x in range(4) for y in range(4) for core in range(2)]


def dot(left, right, left_dim, right_dim):
    return lax.dot_general(
        left, right, (((left_dim,), (right_dim,)), ((), ())), preferred_element_type=F32
    )


def peer_order(column):
    return ((column >> 3) & 3) * 32 + (column >> 5) * 8 + (column & 7)


def inner_spread(block, wide, rows_wide):
    shape = (wide, 128) if rows_wide else (128, wide)
    row = lax.broadcasted_iota(jnp.int32, shape, 0)
    col = lax.broadcasted_iota(jnp.int32, shape, 1)
    hit = (row == 4 * peer_order(col) + block) if rows_wide else (col == 4 * peer_order(row) + block)
    return hit.astype(F32).astype(BF)


def outer_spread(block):
    row = lax.broadcasted_iota(jnp.int32, (512, 128), 0)
    col = lax.broadcasted_iota(jnp.int32, (512, 128), 1)
    col = peer_order(col)
    hit = row == 16 * (col // 4) + 4 * block + col % 4
    return hit.astype(F32).astype(BF)


def fill_inner_t(weight_ref, wide_ref):
    for block in range(4):
        wide_ref[:, 128 * block:128 * block + 128] = dot(
            inner_spread(block, 512, True), weight_ref[block], 1, 1
        ).astype(BF)


def fill_inner(weight_ref, wide_ref):
    for block in range(4):
        wide_ref[128 * block:128 * block + 128, :] = dot(
            weight_ref[block], inner_spread(block, 512, False), 1, 0
        ).astype(BF)


def fill_outer(weight_ref, wide_ref):
    for block in range(4):
        wide_ref[:, 128 * block:128 * block + 128] = dot(
            outer_spread(block), weight_ref[block], 1, 0
        ).astype(BF)


def fill_outer_t(weight_ref, wide_ref):
    for block in range(4):
        wide_ref[128 * block:128 * block + 128, :] = dot(
            weight_ref[block], outer_spread(block), 0, 1
        ).astype(BF)


def rows(value):
    return value.reshape(512, value.shape[-1])


def copies(source, target, sems, tile, axis):
    out = []
    for i in range(source.shape[axis] // tile):
        at = (slice(None),) * axis + (pl.ds(tile * i, tile),)
        out.append(pltpu.make_async_copy(source.at[at], target.at[at], sems.at[i]))
    return out


def begin(many):
    for copy in many:
        copy.start()


def finish(many):
    for copy in many:
        copy.wait()


def load(pairs, sems):
    out = [pltpu.make_async_copy(source, target, sems.at[i]) for i, (source, target) in enumerate(pairs)]
    begin(out)
    return out


def head_kernel(
    x_hbm, g_hbm, inner_hbm, outer_hbm, sent_ref,
    x_buf, g_buf, inner_buf, outer_buf, inner_wide, outer_wide, weight_sems, x_sems, g_sems,
):
    tile = x_buf.shape[0] // HEAD_TILES
    weights = load([(inner_hbm, inner_buf), (outer_hbm, outer_buf)], weight_sems)
    x_copies = copies(x_hbm, x_buf, x_sems, tile, 0)
    g_copies = copies(g_hbm, g_buf, g_sems, tile, 0)
    begin(x_copies)
    begin(g_copies)
    finish(weights)
    fill_inner_t(inner_buf, inner_wide)
    fill_outer(outer_buf, outer_wide)
    for part, wide, buf, arriving in ((0, inner_wide, x_buf, x_copies), (1, outer_wide, g_buf, g_copies)):
        for i in range(HEAD_TILES):
            arriving[i].wait()
            mid = dot(wide[...], buf[tile * i:tile * i + tile, :], 1, 1).astype(BF)
            sent_ref[:, 16 * part:16 * part + 16, tile * i:tile * i + tile] = mid.reshape(32, 16, tile)


def activate(pre_ref, hidden_ref, grad_hidden_ref, grad_pre_ref):
    for top in range(0, 512, ROWS):
        band = slice(top, top + ROWS)
        pre = pre_ref[band, :]
        square = pre * pre
        bent = jnp.tanh(pre * (GELU_SCALE + (GELU_SCALE * GELU_CUBE) * square))
        half = 0.5 + 0.5 * bent
        hidden_ref[band, :] = (pre * half).astype(BF)
        rise = 0.5 * GELU_SCALE + (1.5 * GELU_SCALE * GELU_CUBE) * square
        slope = half + pre * (1.0 - bent * bent) * rise
        grad_pre_ref[band, :] = (grad_hidden_ref[band, :] * slope).astype(BF)


def middle_kernel(
    got_ref, outer_hbm, inner_hbm, sent_hbm, kept_hbm,
    outer_buf, inner_buf, sent_buf, pre_ref, grad_hidden_ref, hidden_ref, grad_pre_ref,
    outer_wide, outer_wide_t, inner_wide, inner_wide_t, weight_sems, sent_sems, kept_sem,
):
    tile = got_ref.shape[2] // TILES
    outer_copy, inner_copy = load([(outer_hbm, outer_buf), (inner_hbm, inner_buf)], weight_sems)
    kept_copy = pltpu.make_async_copy(got_ref, kept_hbm, kept_sem)
    kept_copy.start()
    sent_stores = copies(sent_buf, sent_hbm, sent_sems, tile, 2)
    outer_copy.wait()
    fill_outer_t(outer_buf, outer_wide_t)
    fill_outer(outer_buf, outer_wide)
    inner_copy.wait()
    fill_inner_t(inner_buf, inner_wide_t)
    fill_inner(inner_buf, inner_wide)
    def lanes(i):
        return slice(tile * i, tile * i + tile)

    def pre_act(i):
        pre_ref[i % 2] = dot(outer_wide_t[...], rows(got_ref[:, 0:16, lanes(i)]), 1, 0)

    pre_act(0)
    for i in range(TILES):
        grad_hidden_ref[...] = dot(inner_wide[...], rows(got_ref[:, 16:32, lanes(i)]), 1, 0)
        if i + 1 < TILES:
            pre_act(i + 1)
        activate(pre_ref.at[i % 2], hidden_ref, grad_hidden_ref, grad_pre_ref)
        mid = dot(inner_wide_t[...], hidden_ref[...], 1, 0).astype(BF)
        sent_buf[:, 0:16, lanes(i)] = mid.reshape(32, 16, tile)
        grad_perm = dot(outer_wide[...], grad_pre_ref[...], 1, 0).astype(BF)
        sent_buf[:, 16:32, lanes(i)] = grad_perm.reshape(32, 16, tile)
        sent_stores[i].start()
    finish(sent_stores)
    kept_copy.wait()


def pick(total_ref, picked_ref, by_j):
    row = lax.broadcasted_iota(jnp.int32, (16, 128), 0)
    mine = row // 4 if by_j else row % 4
    for peer, device in enumerate(PEERS):
        band = slice(16 * peer, 16 * peer + 16)
        value = total_ref[band, 0:128]
        for block in range(1, 4):
            value = jnp.where(mine == block, total_ref[band, 128 * block:128 * block + 128], value)
        picked_ref[16 * device:16 * device + 16, :] = value


def spread_out(block_ref, slots, at):
    for rank, out_ref in slots:
        first_row = 16 * rank if isinstance(rank, int) else pl.multiple_of(16 * rank, 16)
        out_ref[at:at + 16, :] = block_ref[pl.ds(first_row, 16), :].astype(out_ref.dtype)


def write_outer(total_ref, picked_ref, block_ref, slots, at):
    pick(total_ref, picked_ref, True)
    for j in range(4):
        for b in range(4):
            block_ref[pl.ds(b, 32, stride=4), :] = picked_ref[pl.ds(4 * j + b, 32, stride=16), :]
        spread_out(block_ref, slots, at + 16 * j)


def write_inner(total_ref, picked_ref, block_ref, slots, at):
    pick(total_ref, picked_ref, False)
    for b in range(4):
        block_ref[...] = picked_ref[pl.ds(b, 128, stride=4), :].T
        spread_out(block_ref, slots, at + 16 * b)


def add(total_ref, value, start):
    if start:
        total_ref[...] = value
    else:
        total_ref[...] += value


def early_kernel(
    got_ref, outer_hbm, inner_hbm, mine_ref, own_ref, near_ref, middle_ref, far_ref,
    outer_buf, inner_buf, pre_ref, grad_hidden_ref, hidden_ref, grad_pre_ref, outer_wide_t, inner_wide,
    outer_total, inner_total, picked_ref, block_ref, weight_sems,
):
    tile = got_ref.shape[2] // TILES
    finish(load([(outer_hbm, outer_buf), (inner_hbm, inner_buf)], weight_sems))
    fill_outer_t(outer_buf, outer_wide_t)
    fill_inner(inner_buf, inner_wide)
    for i in range(TILES):
        lanes = slice(tile * i, tile * i + tile)
        first_perm = rows(got_ref[:, 0:16, lanes])
        grad_mid = rows(got_ref[:, 16:32, lanes])
        pre_ref[...] = dot(outer_wide_t[...], first_perm, 1, 0)
        grad_hidden_ref[...] = dot(inner_wide[...], grad_mid, 1, 0)
        activate(pre_ref, hidden_ref, grad_hidden_ref, grad_pre_ref)
        add(outer_total, dot(first_perm, grad_pre_ref[...], 1, 1), i == 0)
        add(inner_total, dot(grad_mid, hidden_ref[...], 1, 1), i == 0)
    slabs = [(own_ref, 0), (near_ref, 0), (middle_ref, 0), (middle_ref, 128)] + [(far_ref, 128 * i) for i in range(4)]
    slots = [(mine_ref[0] ^ i, ref.at[pl.ds(row, 128), :]) for i, (ref, row) in enumerate(slabs)]
    write_outer(outer_total, picked_ref, block_ref, slots, 0)
    write_inner(inner_total, picked_ref, block_ref, slots, 64)


def late_kernel(
    got_hbm, x_hbm, g_hbm, out_ref,
    got_buf, x_buf, g_buf, outer_total, inner_total, picked_ref, block_ref, second_sems, grad_sems, x_sems, g_sems,
):
    tile = x_buf.shape[0] // LATE_TILES
    slots = [(rank, out_ref.at[rank]) for rank in range(8)]
    g_copies = copies(g_hbm, g_buf, g_sems, tile, 0)
    x_copies = copies(x_hbm, x_buf, x_sems, tile, 0)
    second = copies(got_hbm.at[:, 0:16, :], got_buf.at[:, 0:16, :], second_sems, tile, 2)
    grad = copies(got_hbm.at[:, 16:32, :], got_buf.at[:, 16:32, :], grad_sems, tile, 2)
    for i in range(LATE_TILES):
        begin([second[i], g_copies[i]])
    for i in range(LATE_TILES):
        begin([grad[i], x_copies[i]])
    for i in range(LATE_TILES):
        lanes = slice(tile * i, tile * i + tile)
        finish([second[i], g_copies[i]])
        add(outer_total, dot(rows(got_buf[:, 0:16, lanes]), g_buf[lanes, :], 1, 0), i == 0)
    write_outer(outer_total, picked_ref, block_ref, slots, 0)
    for i in range(LATE_TILES):
        lanes = slice(tile * i, tile * i + tile)
        finish([grad[i], x_copies[i]])
        add(inner_total, dot(rows(got_buf[:, 16:32, lanes]), x_buf[lanes, :], 1, 0), i == 0)
    write_inner(inner_total, picked_ref, block_ref, slots, 64)


def tail_kernel(
    got_ref, outer_hbm, inner_hbm, output_hbm, input_grad_hbm,
    output_buf, input_grad_buf, outer_buf, inner_buf, outer_wide, inner_wide, weight_sems, output_sems, input_grad_sems,
):
    tile = output_buf.shape[0] // TILES
    finish(load([(outer_hbm, outer_buf), (inner_hbm, inner_buf)], weight_sems))
    fill_outer(outer_buf, outer_wide)
    fill_inner_t(inner_buf, inner_wide)
    stores = []
    for part, wide, buf, out, sems in (
        (0, outer_wide, output_buf, output_hbm, output_sems),
        (1, inner_wide, input_grad_buf, input_grad_hbm, input_grad_sems),
    ):
        leaving = copies(buf, out, sems, tile, 0)
        stores += leaving
        for i in range(TILES):
            lanes = slice(tile * i, tile * i + tile)
            message = rows(got_ref[:, 16 * part:16 * part + 16, lanes])
            buf[lanes, :] = dot(message, wide[...], 0, 0).astype(BF)
            leaving[i].start()
    finish(stores)


def call(kernel, name, args, outs, specs, out_specs, scratch, flops):
    moved = 2 * sum(a.size for a in args)
    return pl.pallas_call(
        kernel,
        in_specs=specs,
        out_specs=out_specs,
        out_shape=outs,
        scratch_shapes=scratch,
        name=name,
        cost_estimate=pl.CostEstimate(flops=flops, bytes_accessed=moved, transcendentals=0),
        compiler_params=pltpu.CompilerParams(vmem_limit_bytes=24 * 1024 * 1024),
    )(*args)


def body(tokens, inner_one, outer_one, inner_two, outer_two, cotangent):
    tok = tokens.shape[0]
    one = 2 * tok * 512 * 512
    mine = lax.axis_index("dp").astype(jnp.int32).reshape(1)
    tokens, cotangent, inner_one, outer_one, inner_two, outer_two = (
        pltpu.with_memory_space_constraint(value, pltpu.HBM)
        for value in (tokens, cotangent, inner_one, outer_one, inner_two, outer_two)
    )
    shape = jax.ShapeDtypeStruct
    hbm = pl.BlockSpec(memory_space=pltpu.HBM)
    vmem = pl.BlockSpec(memory_space=pltpu.VMEM)
    smem = pl.BlockSpec(memory_space=pltpu.SMEM)
    weight = pltpu.VMEM((4, 128, 128), BF)
    by_token = pltpu.VMEM((tok, 512), BF)
    by_message = pltpu.VMEM((32, 32, tok), BF)
    wide = pltpu.VMEM((512, 512), BF)
    total = pltpu.VMEM((512, 512), F32)
    picked_part = pltpu.VMEM((512, 128), F32)
    block = pltpu.VMEM((128, 128), F32)
    tile_f32 = pltpu.VMEM((512, tok // TILES), F32)
    tile_bf = pltpu.VMEM((512, tok // TILES), BF)
    pair = pltpu.SemaphoreType.DMA((2,))
    sems = pltpu.SemaphoreType.DMA((TILES,))
    head_sems = pltpu.SemaphoreType.DMA((HEAD_TILES,))
    late_sems = pltpu.SemaphoreType.DMA((LATE_TILES,))

    def exchange(value, axis, order=None):
        return lax.all_to_all(
            value, axis, split_axis=0, concat_axis=0, tiled=True, axis_index_groups=order
        )

    def across(value, flip):
        return lax.ppermute(value, "dp", [(rank, rank ^ flip) for rank in range(8)])

    sent = call(
        head_kernel, "head", (tokens, cotangent, inner_one, outer_two), [by_message], [hbm] * 4, [vmem],
        [by_token, by_token, weight, weight, wide, wide, pair, head_sems, head_sems], 2 * one,
    )[0]
    got = exchange(sent, "mp", [PEERS])
    sent_two, kept = call(
        middle_kernel, "middle", (got, outer_one, inner_two), [pltpu.HBM((32, 32, tok), BF)] * 2, [vmem, hbm, hbm], [hbm] * 2,
        [weight, weight, by_message, pltpu.VMEM((2, 512, tok // TILES), F32), tile_f32, tile_bf, tile_bf, wide, wide, wide, wide, pair, sems, pltpu.SemaphoreType.DMA], 4 * one,
    )
    got_two = exchange(sent_two, "mp", [PEERS])
    own, near, middle, far = call(
        early_kernel, "early_grads", (kept, outer_one, inner_two, mine),
        [shape((128 * n, 128), F32) for n in (1, 1, 2, 4)], [vmem, hbm, hbm, smem], [vmem] * 4,
        [weight, weight, tile_f32, tile_f32, tile_bf, tile_bf, wide, wide, total, total, picked_part, block, pair], 4 * one,
    )
    halves = across(far, 4)
    quarters = across(middle + halves[256:], 2)
    eighth = across(near + halves[128:256] + quarters[128:], 1)
    got_two = pltpu.with_memory_space_constraint(got_two, pltpu.HBM)
    late = call(
        late_kernel, "late_grads", (got_two, tokens, cotangent), [shape((8, 128, 128), BF)], [hbm] * 3, [vmem],
        [by_message, by_token, by_token, total, total, picked_part, block] + [late_sems] * 4, 2 * one,
    )[0]
    late = exchange(late, "dp")
    output, input_grad = call(
        tail_kernel, "tail", (got_two, outer_two, inner_one), [pltpu.HBM((tok, 512), BF)] * 2, [vmem, hbm, hbm], [hbm] * 2,
        [by_token, by_token, weight, weight, wide, wide, pair, sems, sems], 2 * one,
    )
    return (
        output,
        input_grad,
        jnp.sum(late[:, 64:], axis=0, dtype=F32).reshape(4, 16, 128),
        (own[:64] + halves[:64] + quarters[:64] + eighth[:64]).reshape(4, 16, 128),
        (own[64:] + halves[64:128] + quarters[64:128] + eighth[64:]).reshape(4, 16, 128),
        jnp.sum(late[:, :64], axis=0, dtype=F32).reshape(4, 16, 128),
    )


def solution(mesh):
    placed = (
        P("dp", "mp"),
        P("mp", None, None),
        P("mp", None, None),
        P("mp", None, None),
        P("mp", None, None),
        P("dp", "mp"),
    )
    return jax.shard_map(
        body,
        mesh=mesh,
        in_specs=placed,
        out_specs=(
            P("dp", "mp"),
            P("dp", "mp"),
            P("mp", "dp", None),
            P("mp", "dp", None),
            P("mp", "dp", None),
            P("mp", "dp", None),
        ),
        check_vma=False,
    )
```

```python
import jax
import jax.numpy as jnp
from jax import lax
from jax.experimental import pallas as pl
from jax.experimental.pallas import tpu as pltpu
from jax.sharding import PartitionSpec as P

BF = jnp.bfloat16
F32 = jnp.float32
GELU_SCALE = 0.7978845608028654
GELU_CUBE = 0.044715
HEAD_TILES = 1
TILES = 4
LATE_TILES = 4
ROWS = 64


def dot(left, right, left_dim, right_dim):
    return lax.dot_general(
        left, right, (((left_dim,), (right_dim,)), ((), ())), preferred_element_type=F32
    )


def one_hot(shape, place):
    row = lax.broadcasted_iota(jnp.int32, shape, 0)
    col = lax.broadcasted_iota(jnp.int32, shape, 1)
    return place(row, col).astype(F32).astype(BF)


def fill_first(weight_ref, pair_ref):
    for block in range(4):
        at = block % 2
        spread = one_hot((256, 128), lambda row, col: row == 2 * col + at)
        pair_ref[block // 2, :, 128 * at:128 * at + 128] = dot(spread, weight_ref[block], 1, 1).astype(BF)


def fill_second(weight_ref, pair_ref):
    for block in range(4):
        at = block % 2
        spread = one_hot((256, 128), lambda row, col: row == 8 * (col // 4) + 4 * at + col % 4)
        pair_ref[block // 2, :, 128 * at:128 * at + 128] = dot(spread, weight_ref[block], 1, 0).astype(BF)


def outer_spread(block):
    def place(row, col):
        b = col % 4
        return row == 16 * (col // 4) + 8 * (b // 2) + 2 * block + b % 2

    return one_hot((512, 128), place)


def fill_outer(weight_ref, wide_ref):
    for block in range(4):
        wide_ref[:, 128 * block:128 * block + 128] = dot(outer_spread(block), weight_ref[block], 1, 0).astype(BF)


def fill_outer_t(weight_ref, wide_ref):
    for block in range(4):
        wide_ref[128 * block:128 * block + 128, :] = dot(weight_ref[block], outer_spread(block), 0, 1).astype(BF)


def fill_inner(weight_ref, wide_ref):
    for block in range(4):
        spread = one_hot((128, 512), lambda row, col: col == 4 * row + block)
        wide_ref[128 * block:128 * block + 128, :] = dot(weight_ref[block], spread, 1, 0).astype(BF)


def fill_inner_t(weight_ref, wide_ref):
    for block in range(4):
        spread = one_hot((512, 128), lambda row, col: row == 4 * col + block)
        wide_ref[:, 128 * block:128 * block + 128] = dot(spread, weight_ref[block], 1, 1).astype(BF)


def paired(pair_ref, values, right_dim):
    halves = []
    for half in range(2):
        part = values(slice(256 * half, 256 * half + 256))
        product = dot(pair_ref[half], part, 1, right_dim)
        halves.append(product.reshape(32, 8, product.shape[1]))
    return jnp.concatenate(halves, axis=1).astype(BF)


def rows(value):
    return value.reshape(512, value.shape[-1])


def copies(source, target, sems, tile, axis):
    out = []
    for i in range(source.shape[axis] // tile):
        at = (slice(None),) * axis + (pl.ds(tile * i, tile),)
        out.append(pltpu.make_async_copy(source.at[at], target.at[at], sems.at[i]))
    return out


def begin(many):
    for copy in many:
        copy.start()


def finish(many):
    for copy in many:
        copy.wait()


def load(pairs, sems):
    out = [pltpu.make_async_copy(source, target, sems.at[i]) for i, (source, target) in enumerate(pairs)]
    begin(out)
    return out


def head_kernel(
    x_hbm, g_hbm, inner_hbm, outer_hbm, sent_ref,
    x_buf, g_buf, inner_buf, outer_buf, inner_pair, outer_pair, weight_sems, x_sems, g_sems,
):
    tile = x_buf.shape[0] // HEAD_TILES
    weights = load([(inner_hbm, inner_buf), (outer_hbm, outer_buf)], weight_sems)
    x_copies = copies(x_hbm, x_buf, x_sems, tile, 0)
    g_copies = copies(g_hbm, g_buf, g_sems, tile, 0)
    begin(x_copies)
    begin(g_copies)
    finish(weights)
    fill_first(inner_buf, inner_pair)
    fill_second(outer_buf, outer_pair)
    for part, pair_ref, buf, arriving in ((0, inner_pair, x_buf, x_copies), (1, outer_pair, g_buf, g_copies)):
        for i in range(HEAD_TILES):
            arriving[i].wait()
            lanes = slice(tile * i, tile * i + tile)
            sent_ref[:, 16 * part:16 * part + 16, lanes] = paired(pair_ref, lambda at: buf[lanes, at], 1)


def activate(pre_ref, hidden_ref, grad_hidden_ref, grad_pre_ref):
    for top in range(0, 512, ROWS):
        band = slice(top, top + ROWS)
        pre = pre_ref[band, :]
        square = pre * pre
        bent = jnp.tanh(pre * (GELU_SCALE + (GELU_SCALE * GELU_CUBE) * square))
        half = 0.5 + 0.5 * bent
        hidden_ref[band, :] = (pre * half).astype(BF)
        rise = 0.5 * GELU_SCALE + (1.5 * GELU_SCALE * GELU_CUBE) * square
        slope = half + pre * (1.0 - bent * bent) * rise
        grad_pre_ref[band, :] = (grad_hidden_ref[band, :] * slope).astype(BF)


def middle_kernel(
    got_ref, outer_hbm, inner_hbm, sent_hbm, kept_hbm,
    outer_buf, inner_buf, sent_buf, pre_ref, grad_hidden_ref, hidden_ref, grad_pre_ref,
    outer_wide_t, inner_wide, inner_pair, outer_pair, weight_sems, sent_sems, kept_sem,
):
    tile = got_ref.shape[2] // TILES
    outer_copy, inner_copy = load([(outer_hbm, outer_buf), (inner_hbm, inner_buf)], weight_sems)
    kept_copy = pltpu.make_async_copy(got_ref, kept_hbm, kept_sem)
    kept_copy.start()
    sent_stores = copies(sent_buf, sent_hbm, sent_sems, tile, 2)
    outer_copy.wait()
    fill_outer_t(outer_buf, outer_wide_t)
    fill_second(outer_buf, outer_pair)
    inner_copy.wait()
    fill_first(inner_buf, inner_pair)
    fill_inner(inner_buf, inner_wide)
    def lanes(i):
        return slice(tile * i, tile * i + tile)

    def pre_act(i):
        pre_ref[i % 2] = dot(outer_wide_t[...], rows(got_ref[:, 0:16, lanes(i)]), 1, 0)

    pre_act(0)
    for i in range(TILES):
        grad_hidden_ref[...] = dot(inner_wide[...], rows(got_ref[:, 16:32, lanes(i)]), 1, 0)
        if i + 1 < TILES:
            pre_act(i + 1)
        activate(pre_ref.at[i % 2], hidden_ref, grad_hidden_ref, grad_pre_ref)
        sent_buf[:, 0:16, lanes(i)] = paired(inner_pair, lambda at: hidden_ref[at, :], 0)
        sent_buf[:, 16:32, lanes(i)] = paired(outer_pair, lambda at: grad_pre_ref[at, :], 0)
        sent_stores[i].start()
    finish(sent_stores)
    kept_copy.wait()


def picked(total_ref, forward):
    row = lax.broadcasted_iota(jnp.int32, (512, 128), 0)
    mine = (row // 2) % 4 if forward else row % 4
    value = total_ref[:, 0:128]
    for block in range(1, 4):
        value = jnp.where(mine == block, total_ref[:, 128 * block:128 * block + 128], value)
    return value


def spread_out(block_ref, slots, at):
    for rank, out_ref in slots:
        first_row = 16 * rank if isinstance(rank, int) else pl.multiple_of(16 * rank, 16)
        out_ref[at:at + 16, :] = block_ref[pl.ds(first_row, 16), :].astype(out_ref.dtype)


def write_outer(total_ref, picked_ref, block_ref, slots, at):
    picked_ref[...] = picked(total_ref, True)
    for j in range(4):
        for b in range(4):
            row = 8 * (b // 2) + 2 * j + b % 2
            block_ref[pl.ds(b, 32, stride=4), :] = picked_ref[pl.ds(row, 32, stride=16), :]
        spread_out(block_ref, slots, at + 16 * j)


def write_inner(total_ref, picked_ref, block_ref, slots, at):
    picked_ref[...] = picked(total_ref, False)
    for b in range(4):
        block_ref[...] = picked_ref[pl.ds(b, 128, stride=4), :].T
        spread_out(block_ref, slots, at + 16 * b)


def add(total_ref, value, start):
    if start:
        total_ref[...] = value
    else:
        total_ref[...] += value


def early_kernel(
    got_ref, outer_hbm, inner_hbm, mine_ref, own_ref, near_ref, middle_ref, far_ref,
    outer_buf, inner_buf, pre_ref, grad_hidden_ref, hidden_ref, grad_pre_ref, outer_wide_t, inner_wide,
    outer_total, inner_total, picked_ref, block_ref, weight_sems,
):
    tile = got_ref.shape[2] // TILES
    finish(load([(outer_hbm, outer_buf), (inner_hbm, inner_buf)], weight_sems))
    fill_outer_t(outer_buf, outer_wide_t)
    fill_inner(inner_buf, inner_wide)
    for i in range(TILES):
        lanes = slice(tile * i, tile * i + tile)
        first_perm = rows(got_ref[:, 0:16, lanes])
        grad_mid = rows(got_ref[:, 16:32, lanes])
        pre_ref[...] = dot(outer_wide_t[...], first_perm, 1, 0)
        grad_hidden_ref[...] = dot(inner_wide[...], grad_mid, 1, 0)
        activate(pre_ref, hidden_ref, grad_hidden_ref, grad_pre_ref)
        add(outer_total, dot(first_perm, grad_pre_ref[...], 1, 1), i == 0)
        add(inner_total, dot(grad_mid, hidden_ref[...], 1, 1), i == 0)
    slabs = [(own_ref, 0), (near_ref, 0), (middle_ref, 0), (middle_ref, 128)] + [(far_ref, 128 * i) for i in range(4)]
    slots = [(mine_ref[0] ^ i, ref.at[pl.ds(row, 128), :]) for i, (ref, row) in enumerate(slabs)]
    write_outer(outer_total, picked_ref, block_ref, slots, 0)
    write_inner(inner_total, picked_ref, block_ref, slots, 64)


def late_kernel(
    got_hbm, x_hbm, g_hbm, out_ref,
    got_buf, x_buf, g_buf, outer_total, inner_total, picked_ref, block_ref, second_sems, grad_sems, x_sems, g_sems,
):
    tile = x_buf.shape[0] // LATE_TILES
    slots = [(rank, out_ref.at[rank]) for rank in range(8)]
    g_copies = copies(g_hbm, g_buf, g_sems, tile, 0)
    x_copies = copies(x_hbm, x_buf, x_sems, tile, 0)
    second = copies(got_hbm.at[:, 0:16, :], got_buf.at[:, 0:16, :], second_sems, tile, 2)
    grad = copies(got_hbm.at[:, 16:32, :], got_buf.at[:, 16:32, :], grad_sems, tile, 2)
    for i in range(LATE_TILES):
        begin([second[i], g_copies[i]])
    for i in range(LATE_TILES):
        begin([grad[i], x_copies[i]])
    for i in range(LATE_TILES):
        lanes = slice(tile * i, tile * i + tile)
        finish([second[i], g_copies[i]])
        add(outer_total, dot(rows(got_buf[:, 0:16, lanes]), g_buf[lanes, :], 1, 0), i == 0)
    write_outer(outer_total, picked_ref, block_ref, slots, 0)
    for i in range(LATE_TILES):
        lanes = slice(tile * i, tile * i + tile)
        finish([grad[i], x_copies[i]])
        add(inner_total, dot(rows(got_buf[:, 16:32, lanes]), x_buf[lanes, :], 1, 0), i == 0)
    write_inner(inner_total, picked_ref, block_ref, slots, 64)


def tail_kernel(
    got_ref, outer_hbm, inner_hbm, output_hbm, input_grad_hbm,
    output_buf, input_grad_buf, outer_buf, inner_buf, outer_wide, inner_wide, weight_sems, output_sems, input_grad_sems,
):
    tile = output_buf.shape[0] // TILES
    finish(load([(outer_hbm, outer_buf), (inner_hbm, inner_buf)], weight_sems))
    fill_outer(outer_buf, outer_wide)
    fill_inner_t(inner_buf, inner_wide)
    stores = []
    for part, wide, buf, out, sems in (
        (0, outer_wide, output_buf, output_hbm, output_sems),
        (1, inner_wide, input_grad_buf, input_grad_hbm, input_grad_sems),
    ):
        leaving = copies(buf, out, sems, tile, 0)
        stores += leaving
        for i in range(TILES):
            lanes = slice(tile * i, tile * i + tile)
            message = rows(got_ref[:, 16 * part:16 * part + 16, lanes])
            buf[lanes, :] = dot(message, wide[...], 0, 0).astype(BF)
            leaving[i].start()
    finish(stores)


def call(kernel, name, args, outs, specs, out_specs, scratch, flops):
    moved = 2 * sum(a.size for a in args)
    return pl.pallas_call(
        kernel,
        in_specs=specs,
        out_specs=out_specs,
        out_shape=outs,
        scratch_shapes=scratch,
        name=name,
        cost_estimate=pl.CostEstimate(flops=flops, bytes_accessed=moved, transcendentals=0),
        compiler_params=pltpu.CompilerParams(vmem_limit_bytes=24 * 1024 * 1024),
    )(*args)


def body(tokens, inner_one, outer_one, inner_two, outer_two, cotangent):
    tok = tokens.shape[0]
    one = 2 * tok * 512 * 512
    mine = lax.axis_index("dp").astype(jnp.int32).reshape(1)
    tokens, cotangent, inner_one, outer_one, inner_two, outer_two = (
        pltpu.with_memory_space_constraint(value, pltpu.HBM)
        for value in (tokens, cotangent, inner_one, outer_one, inner_two, outer_two)
    )
    shape = jax.ShapeDtypeStruct
    hbm = pl.BlockSpec(memory_space=pltpu.HBM)
    vmem = pl.BlockSpec(memory_space=pltpu.VMEM)
    smem = pl.BlockSpec(memory_space=pltpu.SMEM)
    weight = pltpu.VMEM((4, 128, 128), BF)
    by_token = pltpu.VMEM((tok, 512), BF)
    by_message = pltpu.VMEM((32, 32, tok), BF)
    wide = pltpu.VMEM((512, 512), BF)
    halves_of = pltpu.VMEM((2, 256, 256), BF)
    total = pltpu.VMEM((512, 512), F32)
    picked_part = pltpu.VMEM((512, 128), F32)
    block = pltpu.VMEM((128, 128), F32)
    tile_f32 = pltpu.VMEM((512, tok // TILES), F32)
    tile_bf = pltpu.VMEM((512, tok // TILES), BF)
    pair = pltpu.SemaphoreType.DMA((2,))
    sems = pltpu.SemaphoreType.DMA((TILES,))
    head_sems = pltpu.SemaphoreType.DMA((HEAD_TILES,))
    late_sems = pltpu.SemaphoreType.DMA((LATE_TILES,))

    def exchange(value, axis):
        return lax.all_to_all(value, axis, split_axis=0, concat_axis=0, tiled=True)

    def across(value, flip):
        return lax.ppermute(value, "dp", [(rank, rank ^ flip) for rank in range(8)])

    sent = call(
        head_kernel, "head", (tokens, cotangent, inner_one, outer_two), [by_message], [hbm] * 4, [vmem],
        [by_token, by_token, weight, weight, halves_of, halves_of, pair, head_sems, head_sems], 2 * one,
    )[0]
    got = exchange(sent, "mp")
    sent_two, kept = call(
        middle_kernel, "middle", (got, outer_one, inner_two), [pltpu.HBM((32, 32, tok), BF)] * 2, [vmem, hbm, hbm], [hbm] * 2,
        [weight, weight, by_message, pltpu.VMEM((2, 512, tok // TILES), F32), tile_f32, tile_bf, tile_bf, wide, wide, halves_of, halves_of, pair, sems, pltpu.SemaphoreType.DMA], 4 * one,
    )
    got_two = exchange(sent_two, "mp")
    own, near, middle, far = call(
        early_kernel, "early_grads", (kept, outer_one, inner_two, mine),
        [shape((128 * n, 128), F32) for n in (1, 1, 2, 4)], [vmem, hbm, hbm, smem], [vmem] * 4,
        [weight, weight, tile_f32, tile_f32, tile_bf, tile_bf, wide, wide, total, total, picked_part, block, pair], 4 * one,
    )
    halves = across(far, 4)
    quarters = across(middle + halves[256:], 2)
    eighth = across(near + halves[128:256] + quarters[128:], 1)
    got_two = pltpu.with_memory_space_constraint(got_two, pltpu.HBM)
    late = call(
        late_kernel, "late_grads", (got_two, tokens, cotangent), [shape((8, 128, 128), BF)], [hbm] * 3, [vmem],
        [by_message, by_token, by_token, total, total, picked_part, block] + [late_sems] * 4, 2 * one,
    )[0]
    late = exchange(late, "dp")
    output, input_grad = call(
        tail_kernel, "tail", (got_two, outer_two, inner_one), [pltpu.HBM((tok, 512), BF)] * 2, [vmem, hbm, hbm], [hbm] * 2,
        [by_token, by_token, weight, weight, wide, wide, pair, sems, sems], 2 * one,
    )
    return (
        output,
        input_grad,
        jnp.sum(late[:, 64:], axis=0, dtype=F32).reshape(4, 16, 128),
        (own[:64] + halves[:64] + quarters[:64] + eighth[:64]).reshape(4, 16, 128),
        (own[64:] + halves[64:128] + quarters[64:128] + eighth[64:]).reshape(4, 16, 128),
        jnp.sum(late[:, :64], axis=0, dtype=F32).reshape(4, 16, 128),
    )


def solution(mesh):
    placed = (
        P("dp", "mp"),
        P("mp", None, None),
        P("mp", None, None),
        P("mp", None, None),
        P("mp", None, None),
        P("dp", "mp"),
    )
    return jax.shard_map(
        body,
        mesh=mesh,
        in_specs=placed,
        out_specs=(
            P("dp", "mp"),
            P("dp", "mp"),
            P("mp", "dp", None),
            P("mp", "dp", None),
            P("mp", "dp", None),
            P("mp", "dp", None),
        ),
        check_vma=False,
    )
```

```python
import jax
import jax.numpy as jnp
from jax import lax
from jax.experimental import pallas as pl
from jax.experimental.pallas import tpu as pltpu
from jax.sharding import PartitionSpec as P

BF = jnp.bfloat16
F32 = jnp.float32
GELU_SCALE = 0.7978845608028654
GELU_CUBE = 0.044715
HEAD_TILES = 1
TILES = 4
LATE_TILES = 4
ROWS = 64


def dot(left, right, left_dim, right_dim):
    return lax.dot_general(
        left, right, (((left_dim,), (right_dim,)), ((), ())), preferred_element_type=F32
    )


def one_hot(shape, place):
    row = lax.broadcasted_iota(jnp.int32, shape, 0)
    col = lax.broadcasted_iota(jnp.int32, shape, 1)
    return place(row, col).astype(F32).astype(BF)


def fill_first(weight_ref, pair_ref):
    for block in range(4):
        at = block % 2
        spread = one_hot((256, 128), lambda row, col: row == 2 * col + at)
        pair_ref[block // 2, :, 128 * at:128 * at + 128] = dot(spread, weight_ref[block], 1, 1).astype(BF)


def fill_second(weight_ref, pair_ref):
    for block in range(4):
        at = block % 2
        spread = one_hot((256, 128), lambda row, col: row == 8 * (col // 4) + 4 * at + col % 4)
        pair_ref[block // 2, :, 128 * at:128 * at + 128] = dot(spread, weight_ref[block], 1, 0).astype(BF)


def outer_spread(block):
    def place(row, col):
        b = col % 4
        return row == 16 * (col // 4) + 8 * (b // 2) + 2 * block + b % 2

    return one_hot((512, 128), place)


def fill_outer(weight_ref, wide_ref):
    for block in range(4):
        wide_ref[:, 128 * block:128 * block + 128] = dot(outer_spread(block), weight_ref[block], 1, 0).astype(BF)


def fill_outer_t(weight_ref, wide_ref):
    for block in range(4):
        wide_ref[128 * block:128 * block + 128, :] = dot(weight_ref[block], outer_spread(block), 0, 1).astype(BF)


def fill_inner(weight_ref, wide_ref):
    for block in range(4):
        spread = one_hot((128, 512), lambda row, col: col == 4 * row + block)
        wide_ref[128 * block:128 * block + 128, :] = dot(weight_ref[block], spread, 1, 0).astype(BF)


def fill_inner_t(weight_ref, wide_ref):
    for block in range(4):
        spread = one_hot((512, 128), lambda row, col: row == 4 * col + block)
        wide_ref[:, 128 * block:128 * block + 128] = dot(spread, weight_ref[block], 1, 1).astype(BF)


def paired(pair_ref, values, right_dim):
    halves = []
    for half in range(2):
        part = values(slice(256 * half, 256 * half + 256))
        product = dot(pair_ref[half], part, 1, right_dim)
        halves.append(product.reshape(32, 8, product.shape[1]))
    return jnp.concatenate(halves, axis=1).astype(BF)


def rows(value):
    return value.reshape(512, value.shape[-1])


def copies(source, target, sems, tile, axis):
    out = []
    for i in range(source.shape[axis] // tile):
        at = (slice(None),) * axis + (pl.ds(tile * i, tile),)
        out.append(pltpu.make_async_copy(source.at[at], target.at[at], sems.at[i]))
    return out


def begin(many):
    for copy in many:
        copy.start()


def finish(many):
    for copy in many:
        copy.wait()


def load(pairs, sems):
    out = [pltpu.make_async_copy(source, target, sems.at[i]) for i, (source, target) in enumerate(pairs)]
    begin(out)
    return out


def head_kernel(
    x_hbm, g_hbm, inner_hbm, outer_hbm, sent_ref,
    x_buf, g_buf, inner_buf, outer_buf, inner_pair, outer_pair, weight_sems, x_sems, g_sems,
):
    tile = x_buf.shape[0] // HEAD_TILES
    weights = load([(inner_hbm, inner_buf), (outer_hbm, outer_buf)], weight_sems)
    x_copies = copies(x_hbm, x_buf, x_sems, tile, 0)
    g_copies = copies(g_hbm, g_buf, g_sems, tile, 0)
    begin(x_copies)
    begin(g_copies)
    finish(weights)
    fill_first(inner_buf, inner_pair)
    fill_second(outer_buf, outer_pair)
    for part, pair_ref, buf, arriving in ((0, inner_pair, x_buf, x_copies), (1, outer_pair, g_buf, g_copies)):
        for i in range(HEAD_TILES):
            arriving[i].wait()
            lanes = slice(tile * i, tile * i + tile)
            sent_ref[:, 16 * part:16 * part + 16, lanes] = paired(pair_ref, lambda at: buf[lanes, at], 1)


def activate(pre_ref, hidden_ref, grad_hidden_ref, grad_pre_ref):
    for top in range(0, 512, ROWS):
        band = slice(top, top + ROWS)
        pre = pre_ref[band, :]
        square = pre * pre
        bent = jnp.tanh(pre * (GELU_SCALE + (GELU_SCALE * GELU_CUBE) * square))
        half = 0.5 + 0.5 * bent
        hidden_ref[band, :] = (pre * half).astype(BF)
        rise = 0.5 * GELU_SCALE + (1.5 * GELU_SCALE * GELU_CUBE) * square
        slope = half + pre * (1.0 - bent * bent) * rise
        grad_pre_ref[band, :] = (grad_hidden_ref[band, :] * slope).astype(BF)


def middle_kernel(
    got_ref, outer_hbm, inner_hbm, sent_hbm, kept_hbm,
    outer_buf, inner_buf, sent_buf, pre_ref, grad_hidden_ref, hidden_ref, grad_pre_ref,
    outer_wide_t, inner_wide, inner_pair, outer_pair, weight_sems, sent_sems, kept_sem,
):
    tile = got_ref.shape[2] // TILES
    outer_copy, inner_copy = load([(outer_hbm, outer_buf), (inner_hbm, inner_buf)], weight_sems)
    kept_copy = pltpu.make_async_copy(got_ref, kept_hbm, kept_sem)
    kept_copy.start()
    sent_stores = copies(sent_buf, sent_hbm, sent_sems, tile, 2)
    outer_copy.wait()
    fill_outer_t(outer_buf, outer_wide_t)
    fill_second(outer_buf, outer_pair)
    inner_copy.wait()
    fill_first(inner_buf, inner_pair)
    fill_inner(inner_buf, inner_wide)
    def lanes(i):
        return slice(tile * i, tile * i + tile)

    def pre_act(i):
        pre_ref[i % 2] = dot(outer_wide_t[...], rows(got_ref[:, 0:16, lanes(i)]), 1, 0)

    pre_act(0)
    for i in range(TILES):
        grad_hidden_ref[...] = dot(inner_wide[...], rows(got_ref[:, 16:32, lanes(i)]), 1, 0)
        if i + 1 < TILES:
            pre_act(i + 1)
        activate(pre_ref.at[i % 2], hidden_ref, grad_hidden_ref, grad_pre_ref)
        sent_buf[:, 0:16, lanes(i)] = paired(inner_pair, lambda at: hidden_ref[at, :], 0)
        sent_buf[:, 16:32, lanes(i)] = paired(outer_pair, lambda at: grad_pre_ref[at, :], 0)
        sent_stores[i].start()
    finish(sent_stores)
    kept_copy.wait()


def picked(total_ref, forward):
    row = lax.broadcasted_iota(jnp.int32, (512, 128), 0)
    mine = (row // 2) % 4 if forward else row % 4
    value = total_ref[:, 0:128]
    for block in range(1, 4):
        value = jnp.where(mine == block, total_ref[:, 128 * block:128 * block + 128], value)
    return value


def spread_out(block_ref, slots, at):
    for rank, out_ref in slots:
        first_row = 16 * rank if isinstance(rank, int) else pl.multiple_of(16 * rank, 16)
        out_ref[at:at + 16, :] = block_ref[pl.ds(first_row, 16), :].astype(out_ref.dtype)


def write_outer(total_ref, picked_ref, block_ref, slots, at):
    picked_ref[...] = picked(total_ref, True)
    for j in range(4):
        for b in range(4):
            row = 8 * (b // 2) + 2 * j + b % 2
            block_ref[pl.ds(b, 32, stride=4), :] = picked_ref[pl.ds(row, 32, stride=16), :]
        spread_out(block_ref, slots, at + 16 * j)


def write_inner(total_ref, picked_ref, block_ref, slots, at):
    picked_ref[...] = picked(total_ref, False)
    for b in range(4):
        block_ref[...] = picked_ref[pl.ds(b, 128, stride=4), :].T
        spread_out(block_ref, slots, at + 16 * b)


def add(total_ref, value, start):
    if start:
        total_ref[...] = value
    else:
        total_ref[...] += value


def early_kernel(
    got_ref, outer_hbm, inner_hbm, mine_ref, own_ref, near_ref, middle_ref, far_ref,
    outer_buf, inner_buf, pre_ref, grad_hidden_ref, hidden_ref, grad_pre_ref, outer_wide_t, inner_wide,
    outer_total, inner_total, picked_ref, block_ref, weight_sems,
):
    tile = got_ref.shape[2] // TILES
    finish(load([(outer_hbm, outer_buf), (inner_hbm, inner_buf)], weight_sems))
    fill_outer_t(outer_buf, outer_wide_t)
    fill_inner(inner_buf, inner_wide)
    for i in range(TILES):
        lanes = slice(tile * i, tile * i + tile)
        first_perm = rows(got_ref[:, 0:16, lanes])
        grad_mid = rows(got_ref[:, 16:32, lanes])
        pre_ref[...] = dot(outer_wide_t[...], first_perm, 1, 0)
        grad_hidden_ref[...] = dot(inner_wide[...], grad_mid, 1, 0)
        activate(pre_ref, hidden_ref, grad_hidden_ref, grad_pre_ref)
        add(outer_total, dot(first_perm, grad_pre_ref[...], 1, 1), i == 0)
        add(inner_total, dot(grad_mid, hidden_ref[...], 1, 1), i == 0)
    slabs = [(own_ref, 0), (near_ref, 0), (middle_ref, 0), (middle_ref, 128)] + [(far_ref, 128 * i) for i in range(4)]
    slots = [(mine_ref[0] ^ i, ref.at[pl.ds(row, 128), :]) for i, (ref, row) in enumerate(slabs)]
    write_outer(outer_total, picked_ref, block_ref, slots, 0)
    write_inner(inner_total, picked_ref, block_ref, slots, 64)


def fetch_kernel(x_hbm, x_ref, sem):
    copy = pltpu.make_async_copy(x_hbm, x_ref, sem)
    copy.start()
    copy.wait()


def late_kernel(
    got_hbm, x_ref, g_hbm, out_ref,
    got_buf, g_buf, outer_total, inner_total, picked_ref, block_ref, second_sems, grad_sems, g_sems,
):
    tile = g_buf.shape[0] // LATE_TILES
    slots = [(rank, out_ref.at[7 - rank]) for rank in range(8)]
    g_copies = copies(g_hbm, g_buf, g_sems, tile, 0)
    second = copies(got_hbm.at[:, 0:16, :], got_buf.at[:, 0:16, :], second_sems, tile, 2)
    grad = copies(got_hbm.at[:, 16:32, :], got_buf.at[:, 16:32, :], grad_sems, tile, 2)
    begin(grad)
    for i in range(LATE_TILES):
        begin([second[i], g_copies[i]])
    for i in range(LATE_TILES):
        lanes = slice(tile * i, tile * i + tile)
        grad[i].wait()
        add(inner_total, dot(rows(got_buf[:, 16:32, lanes]), x_ref[lanes, :], 1, 0), i == 0)
    write_inner(inner_total, picked_ref, block_ref, slots, 64)
    for i in range(LATE_TILES):
        lanes = slice(tile * i, tile * i + tile)
        finish([second[i], g_copies[i]])
        add(outer_total, dot(rows(got_buf[:, 0:16, lanes]), g_buf[lanes, :], 1, 0), i == 0)
    write_outer(outer_total, picked_ref, block_ref, slots, 0)


def tail_kernel(
    got_ref, outer_hbm, inner_hbm, output_hbm, input_grad_hbm,
    output_buf, input_grad_buf, outer_buf, inner_buf, outer_wide, inner_wide, weight_sems, output_sems, input_grad_sems,
):
    tile = output_buf.shape[0] // TILES
    finish(load([(outer_hbm, outer_buf), (inner_hbm, inner_buf)], weight_sems))
    fill_outer(outer_buf, outer_wide)
    fill_inner_t(inner_buf, inner_wide)
    stores = []
    for part, wide, buf, out, sems in (
        (0, outer_wide, output_buf, output_hbm, output_sems),
        (1, inner_wide, input_grad_buf, input_grad_hbm, input_grad_sems),
    ):
        leaving = copies(buf, out, sems, tile, 0)
        stores += leaving
        for i in range(TILES):
            lanes = slice(tile * i, tile * i + tile)
            message = rows(got_ref[:, 16 * part:16 * part + 16, lanes])
            buf[lanes, :] = dot(message, wide[...], 0, 0).astype(BF)
            leaving[i].start()
    finish(stores)


def call(kernel, name, args, outs, specs, out_specs, scratch, flops):
    moved = 2 * sum(a.size for a in args)
    return pl.pallas_call(
        kernel,
        in_specs=specs,
        out_specs=out_specs,
        out_shape=outs,
        scratch_shapes=scratch,
        name=name,
        cost_estimate=pl.CostEstimate(flops=flops, bytes_accessed=moved, transcendentals=0),
        compiler_params=pltpu.CompilerParams(vmem_limit_bytes=24 * 1024 * 1024),
    )(*args)


def body(tokens, inner_one, outer_one, inner_two, outer_two, cotangent):
    tok = tokens.shape[0]
    one = 2 * tok * 512 * 512
    mine = lax.axis_index("dp").astype(jnp.int32).reshape(1)
    tokens, cotangent, inner_one, outer_one, inner_two, outer_two = (
        pltpu.with_memory_space_constraint(value, pltpu.HBM)
        for value in (tokens, cotangent, inner_one, outer_one, inner_two, outer_two)
    )
    shape = jax.ShapeDtypeStruct
    hbm = pl.BlockSpec(memory_space=pltpu.HBM)
    vmem = pl.BlockSpec(memory_space=pltpu.VMEM)
    smem = pl.BlockSpec(memory_space=pltpu.SMEM)
    weight = pltpu.VMEM((4, 128, 128), BF)
    by_token = pltpu.VMEM((tok, 512), BF)
    by_message = pltpu.VMEM((32, 32, tok), BF)
    wide = pltpu.VMEM((512, 512), BF)
    halves_of = pltpu.VMEM((2, 256, 256), BF)
    total = pltpu.VMEM((512, 512), F32)
    picked_part = pltpu.VMEM((512, 128), F32)
    block = pltpu.VMEM((128, 128), F32)
    tile_f32 = pltpu.VMEM((512, tok // TILES), F32)
    tile_bf = pltpu.VMEM((512, tok // TILES), BF)
    pair = pltpu.SemaphoreType.DMA((2,))
    sems = pltpu.SemaphoreType.DMA((TILES,))
    head_sems = pltpu.SemaphoreType.DMA((HEAD_TILES,))
    late_sems = pltpu.SemaphoreType.DMA((LATE_TILES,))

    def exchange(value, axis, order=None):
        return lax.all_to_all(
            value, axis, split_axis=0, concat_axis=0, tiled=True, axis_index_groups=order
        )

    def across(value, flip):
        return lax.ppermute(value, "dp", [(rank, rank ^ flip) for rank in range(8)])

    sent = call(
        head_kernel, "head", (tokens, cotangent, inner_one, outer_two), [by_message], [hbm] * 4, [vmem],
        [by_token, by_token, weight, weight, halves_of, halves_of, pair, head_sems, head_sems], 2 * one,
    )[0]
    got = exchange(sent, "mp")
    sent_two, kept = call(
        middle_kernel, "middle", (got, outer_one, inner_two), [pltpu.HBM((32, 32, tok), BF)] * 2, [vmem, hbm, hbm], [hbm] * 2,
        [weight, weight, by_message, pltpu.VMEM((2, 512, tok // TILES), F32), tile_f32, tile_bf, tile_bf, wide, wide, halves_of, halves_of, pair, sems, pltpu.SemaphoreType.DMA], 4 * one,
    )
    got_two = exchange(sent_two, "mp")
    own, near, middle, far = call(
        early_kernel, "early_grads", (kept, outer_one, inner_two, mine),
        [shape((128 * n, 128), F32) for n in (1, 1, 2, 4)], [vmem, hbm, hbm, smem], [vmem] * 4,
        [weight, weight, tile_f32, tile_f32, tile_bf, tile_bf, wide, wide, total, total, picked_part, block, pair], 4 * one,
    )
    halves = across(far, 4)
    quarters = across(middle + halves[256:], 2)
    eighth = across(near + halves[128:256] + quarters[128:], 1)
    got_two = pltpu.with_memory_space_constraint(got_two, pltpu.HBM)
    tokens_here = call(
        fetch_kernel, "fetch", (tokens,), [by_token], [hbm], [vmem], [pltpu.SemaphoreType.DMA], 0
    )[0]
    late = call(
        late_kernel, "late_grads", (got_two, tokens_here, cotangent), [shape((8, 128, 128), BF)], [hbm, vmem, hbm], [vmem],
        [by_message, by_token, total, total, picked_part, block] + [late_sems] * 3, 2 * one,
    )[0]
    late = exchange(late, "dp", [[7 - rank for rank in range(8)]])
    output, input_grad = call(
        tail_kernel, "tail", (got_two, outer_two, inner_one), [pltpu.HBM((tok, 512), BF)] * 2, [vmem, hbm, hbm], [hbm] * 2,
        [by_token, by_token, weight, weight, wide, wide, pair, sems, sems], 2 * one,
    )
    return (
        output,
        input_grad,
        jnp.sum(late[:, 64:], axis=0, dtype=F32).reshape(4, 16, 128),
        (own[:64] + halves[:64] + quarters[:64] + eighth[:64]).reshape(4, 16, 128),
        (own[64:] + halves[64:128] + quarters[64:128] + eighth[64:]).reshape(4, 16, 128),
        jnp.sum(late[:, :64], axis=0, dtype=F32).reshape(4, 16, 128),
    )


def solution(mesh):
    placed = (
        P("dp", "mp"),
        P("mp", None, None),
        P("mp", None, None),
        P("mp", None, None),
        P("mp", None, None),
        P("dp", "mp"),
    )
    return jax.shard_map(
        body,
        mesh=mesh,
        in_specs=placed,
        out_specs=(
            P("dp", "mp"),
            P("dp", "mp"),
            P("mp", "dp", None),
            P("mp", "dp", None),
            P("mp", "dp", None),
            P("mp", "dp", None),
        ),
        check_vma=False,
    )
```

```python
import jax
import jax.numpy as jnp
from jax import lax
from jax.experimental import pallas as pl
from jax.experimental.pallas import tpu as pltpu
from jax.sharding import PartitionSpec as P

BF = jnp.bfloat16
F32 = jnp.float32
GELU_SCALE = 0.7978845608028654
GELU_CUBE = 0.044715
HEAD_TILES = 1
TILES = 4
LATE_TILES = 4
TAIL_TILES = 2
ROWS = 64


def dot(left, right, left_dim, right_dim):
    return lax.dot_general(
        left, right, (((left_dim,), (right_dim,)), ((), ())), preferred_element_type=F32
    )


def one_hot(shape, place):
    row = lax.broadcasted_iota(jnp.int32, shape, 0)
    col = lax.broadcasted_iota(jnp.int32, shape, 1)
    return place(row, col).astype(F32).astype(BF)


def fill_first(weight_ref, pair_ref):
    for block in range(4):
        at = block % 2
        spread = one_hot((256, 128), lambda row, col: row == 2 * col + at)
        pair_ref[block // 2, :, 128 * at:128 * at + 128] = dot(spread, weight_ref[block], 1, 1).astype(BF)


def fill_second(weight_ref, pair_ref):
    for block in range(4):
        at = block % 2
        spread = one_hot((256, 128), lambda row, col: row == 8 * (col // 4) + 4 * at + col % 4)
        pair_ref[block // 2, :, 128 * at:128 * at + 128] = dot(spread, weight_ref[block], 1, 0).astype(BF)


def outer_spread(block):
    def place(row, col):
        b = col % 4
        return row == 16 * (col // 4) + 8 * (b // 2) + 2 * block + b % 2

    return one_hot((512, 128), place)


def fill_outer(weight_ref, wide_ref):
    for block in range(4):
        wide_ref[:, 128 * block:128 * block + 128] = dot(outer_spread(block), weight_ref[block], 1, 0).astype(BF)


def fill_outer_t(weight_ref, wide_ref):
    for block in range(4):
        wide_ref[128 * block:128 * block + 128, :] = dot(weight_ref[block], outer_spread(block), 0, 1).astype(BF)


def fill_inner(weight_ref, wide_ref):
    for block in range(4):
        spread = one_hot((128, 512), lambda row, col: col == 4 * row + block)
        wide_ref[128 * block:128 * block + 128, :] = dot(weight_ref[block], spread, 1, 0).astype(BF)


def fill_inner_t(weight_ref, wide_ref):
    for block in range(4):
        spread = one_hot((512, 128), lambda row, col: row == 4 * col + block)
        wide_ref[:, 128 * block:128 * block + 128] = dot(spread, weight_ref[block], 1, 1).astype(BF)


def paired(pair_ref, values, right_dim):
    halves = []
    for half in range(2):
        part = values(slice(256 * half, 256 * half + 256))
        product = dot(pair_ref[half], part, 1, right_dim)
        halves.append(product.reshape(32, 8, product.shape[1]))
    return jnp.concatenate(halves, axis=1).astype(BF)


def rows(value):
    return value.reshape(512, value.shape[-1])


def copies(source, target, sems, tile, axis):
    out = []
    for i in range(source.shape[axis] // tile):
        at = (slice(None),) * axis + (pl.ds(tile * i, tile),)
        out.append(pltpu.make_async_copy(source.at[at], target.at[at], sems.at[i]))
    return out


def begin(many):
    for copy in many:
        copy.start()


def finish(many):
    for copy in many:
        copy.wait()


def load(pairs, sems):
    out = [pltpu.make_async_copy(source, target, sems.at[i]) for i, (source, target) in enumerate(pairs)]
    begin(out)
    return out


def head_kernel(
    x_hbm, g_hbm, inner_hbm, outer_hbm, sent_ref,
    x_buf, g_buf, inner_buf, outer_buf, inner_pair, outer_pair, weight_sems, x_sems, g_sems,
):
    tile = x_buf.shape[0] // HEAD_TILES
    weights = load([(inner_hbm, inner_buf), (outer_hbm, outer_buf)], weight_sems)
    x_copies = copies(x_hbm, x_buf, x_sems, tile, 0)
    g_copies = copies(g_hbm, g_buf, g_sems, tile, 0)
    begin(x_copies)
    begin(g_copies)
    finish(weights)
    fill_first(inner_buf, inner_pair)
    fill_second(outer_buf, outer_pair)
    for part, pair_ref, buf, arriving in ((0, inner_pair, x_buf, x_copies), (1, outer_pair, g_buf, g_copies)):
        for i in range(HEAD_TILES):
            arriving[i].wait()
            lanes = slice(tile * i, tile * i + tile)
            sent_ref[:, 16 * part:16 * part + 16, lanes] = paired(pair_ref, lambda at: buf[lanes, at], 1)


def activate(pre_ref, hidden_ref, grad_hidden_ref, grad_pre_ref):
    for top in range(0, 512, ROWS):
        band = slice(top, top + ROWS)
        pre = pre_ref[band, :]
        square = pre * pre
        bent = jnp.tanh(pre * (GELU_SCALE + (GELU_SCALE * GELU_CUBE) * square))
        half = 0.5 + 0.5 * bent
        hidden_ref[band, :] = (pre * half).astype(BF)
        rise = 0.5 * GELU_SCALE + (1.5 * GELU_SCALE * GELU_CUBE) * square
        slope = half + pre * (1.0 - bent * bent) * rise
        grad_pre_ref[band, :] = (grad_hidden_ref[band, :] * slope).astype(BF)


def middle_kernel(
    got_ref, outer_hbm, inner_hbm, sent_hbm, kept_hbm,
    outer_buf, inner_buf, sent_buf, pre_ref, grad_hidden_ref, hidden_ref, grad_pre_ref,
    outer_wide_t, inner_wide, inner_pair, outer_pair, weight_sems, sent_sems, kept_sem,
):
    tile = got_ref.shape[2] // TILES
    outer_copy, inner_copy = load([(outer_hbm, outer_buf), (inner_hbm, inner_buf)], weight_sems)
    kept_copy = pltpu.make_async_copy(got_ref, kept_hbm, kept_sem)
    kept_copy.start()
    sent_stores = copies(sent_buf, sent_hbm, sent_sems, tile, 2)
    outer_copy.wait()
    fill_outer_t(outer_buf, outer_wide_t)
    fill_second(outer_buf, outer_pair)
    inner_copy.wait()
    fill_first(inner_buf, inner_pair)
    fill_inner(inner_buf, inner_wide)
    def lanes(i):
        return slice(tile * i, tile * i + tile)

    def pre_act(i):
        pre_ref[i % 2] = dot(outer_wide_t[...], rows(got_ref[:, 0:16, lanes(i)]), 1, 0)

    pre_act(0)
    for i in range(TILES):
        grad_hidden_ref[...] = dot(inner_wide[...], rows(got_ref[:, 16:32, lanes(i)]), 1, 0)
        if i + 1 < TILES:
            pre_act(i + 1)
        activate(pre_ref.at[i % 2], hidden_ref, grad_hidden_ref, grad_pre_ref)
        sent_buf[:, 0:16, lanes(i)] = paired(inner_pair, lambda at: hidden_ref[at, :], 0)
        sent_buf[:, 16:32, lanes(i)] = paired(outer_pair, lambda at: grad_pre_ref[at, :], 0)
        sent_stores[i].start()
    finish(sent_stores)
    kept_copy.wait()


def picked(total_ref, forward):
    row = lax.broadcasted_iota(jnp.int32, (512, 128), 0)
    mine = (row // 2) % 4 if forward else row % 4
    value = total_ref[:, 0:128]
    for block in range(1, 4):
        value = jnp.where(mine == block, total_ref[:, 128 * block:128 * block + 128], value)
    return value


def spread_out(block_ref, slots, at):
    for rank, out_ref in slots:
        first_row = 16 * rank if isinstance(rank, int) else pl.multiple_of(16 * rank, 16)
        out_ref[at:at + 16, :] = block_ref[pl.ds(first_row, 16), :].astype(out_ref.dtype)


def write_outer(total_ref, picked_ref, block_ref, slots, at):
    picked_ref[...] = picked(total_ref, True)
    for j in range(4):
        for b in range(4):
            row = 8 * (b // 2) + 2 * j + b % 2
            block_ref[pl.ds(b, 32, stride=4), :] = picked_ref[pl.ds(row, 32, stride=16), :]
        spread_out(block_ref, slots, at + 16 * j)


def write_inner(total_ref, picked_ref, block_ref, slots, at):
    picked_ref[...] = picked(total_ref, False)
    for b in range(4):
        block_ref[...] = picked_ref[pl.ds(b, 128, stride=4), :].T
        spread_out(block_ref, slots, at + 16 * b)


def add(total_ref, value, start):
    if start:
        total_ref[...] = value
    else:
        total_ref[...] += value


def early_kernel(
    got_ref, outer_hbm, inner_hbm, mine_ref, own_ref, near_ref, middle_ref, far_ref,
    outer_buf, inner_buf, pre_ref, grad_hidden_ref, hidden_ref, grad_pre_ref, outer_wide_t, inner_wide,
    outer_total, inner_total, picked_ref, block_ref, weight_sems,
):
    tile = got_ref.shape[2] // TILES
    finish(load([(outer_hbm, outer_buf), (inner_hbm, inner_buf)], weight_sems))
    fill_outer_t(outer_buf, outer_wide_t)
    fill_inner(inner_buf, inner_wide)
    for i in range(TILES):
        lanes = slice(tile * i, tile * i + tile)
        first_perm = rows(got_ref[:, 0:16, lanes])
        grad_mid = rows(got_ref[:, 16:32, lanes])
        pre_ref[...] = dot(outer_wide_t[...], first_perm, 1, 0)
        grad_hidden_ref[...] = dot(inner_wide[...], grad_mid, 1, 0)
        activate(pre_ref, hidden_ref, grad_hidden_ref, grad_pre_ref)
        add(outer_total, dot(first_perm, grad_pre_ref[...], 1, 1), i == 0)
        add(inner_total, dot(grad_mid, hidden_ref[...], 1, 1), i == 0)
    slabs = [(own_ref, 0), (near_ref, 0), (middle_ref, 0), (middle_ref, 128)] + [(far_ref, 128 * i) for i in range(4)]
    slots = [(mine_ref[0] ^ i, ref.at[pl.ds(row, 128), :]) for i, (ref, row) in enumerate(slabs)]
    write_outer(outer_total, picked_ref, block_ref, slots, 0)
    write_inner(inner_total, picked_ref, block_ref, slots, 64)


def fetch_kernel(x_hbm, x_ref, sem):
    copy = pltpu.make_async_copy(x_hbm, x_ref, sem)
    copy.start()
    copy.wait()


def late_kernel(
    got_hbm, x_ref, g_hbm, out_ref,
    got_buf, g_buf, outer_total, inner_total, picked_ref, block_ref, second_sems, grad_sems, g_sems,
):
    tile = g_buf.shape[0] // LATE_TILES
    slots = [(rank, out_ref.at[7 - rank]) for rank in range(8)]
    g_copies = copies(g_hbm, g_buf, g_sems, tile, 0)
    second = copies(got_hbm.at[:, 0:16, :], got_buf.at[:, 0:16, :], second_sems, tile, 2)
    grad = copies(got_hbm.at[:, 16:32, :], got_buf.at[:, 16:32, :], grad_sems, tile, 2)
    begin(grad)
    for i in range(LATE_TILES):
        begin([second[i], g_copies[i]])
    for i in range(LATE_TILES):
        lanes = slice(tile * i, tile * i + tile)
        grad[i].wait()
        add(inner_total, dot(rows(got_buf[:, 16:32, lanes]), x_ref[lanes, :], 1, 0), i == 0)
    write_inner(inner_total, picked_ref, block_ref, slots, 64)
    for i in range(LATE_TILES):
        lanes = slice(tile * i, tile * i + tile)
        finish([second[i], g_copies[i]])
        add(outer_total, dot(rows(got_buf[:, 0:16, lanes]), g_buf[lanes, :], 1, 0), i == 0)
    write_outer(outer_total, picked_ref, block_ref, slots, 0)


def tail_kernel(
    got_hbm, outer_hbm, inner_hbm, output_hbm, input_grad_hbm,
    got_buf, output_buf, input_grad_buf, outer_buf, inner_buf, outer_wide, inner_wide,
    weight_sems, got_sems, output_sems, input_grad_sems,
):
    tile = output_buf.shape[0] // TAIL_TILES
    weights = load([(outer_hbm, outer_buf), (inner_hbm, inner_buf)], weight_sems)
    loads = copies(got_hbm, got_buf, got_sems, tile, 2)
    begin(loads)
    finish(weights)
    fill_outer(outer_buf, outer_wide)
    fill_inner_t(inner_buf, inner_wide)
    output_stores = copies(output_buf, output_hbm, output_sems, tile, 0)
    input_grad_stores = copies(input_grad_buf, input_grad_hbm, input_grad_sems, tile, 0)
    for i in range(TAIL_TILES):
        lanes = slice(tile * i, tile * i + tile)
        loads[i].wait()
        output_buf[lanes, :] = dot(rows(got_buf[:, 0:16, lanes]), outer_wide[...], 0, 0).astype(BF)
        output_stores[i].start()
        input_grad_buf[lanes, :] = dot(rows(got_buf[:, 16:32, lanes]), inner_wide[...], 0, 0).astype(BF)
        input_grad_stores[i].start()
    finish(output_stores)
    finish(input_grad_stores)


def call(kernel, name, args, outs, specs, out_specs, scratch, flops):
    moved = 2 * sum(a.size for a in args)
    return pl.pallas_call(
        kernel,
        in_specs=specs,
        out_specs=out_specs,
        out_shape=outs,
        scratch_shapes=scratch,
        name=name,
        cost_estimate=pl.CostEstimate(flops=flops, bytes_accessed=moved, transcendentals=0),
        compiler_params=pltpu.CompilerParams(vmem_limit_bytes=24 * 1024 * 1024),
    )(*args)


def body(tokens, inner_one, outer_one, inner_two, outer_two, cotangent):
    tok = tokens.shape[0]
    one = 2 * tok * 512 * 512
    mine = lax.axis_index("dp").astype(jnp.int32).reshape(1)
    tokens, cotangent, inner_one, outer_one, inner_two, outer_two = (
        pltpu.with_memory_space_constraint(value, pltpu.HBM)
        for value in (tokens, cotangent, inner_one, outer_one, inner_two, outer_two)
    )
    shape = jax.ShapeDtypeStruct
    hbm = pl.BlockSpec(memory_space=pltpu.HBM)
    vmem = pl.BlockSpec(memory_space=pltpu.VMEM)
    smem = pl.BlockSpec(memory_space=pltpu.SMEM)
    weight = pltpu.VMEM((4, 128, 128), BF)
    by_token = pltpu.VMEM((tok, 512), BF)
    by_message = pltpu.VMEM((32, 32, tok), BF)
    wide = pltpu.VMEM((512, 512), BF)
    halves_of = pltpu.VMEM((2, 256, 256), BF)
    total = pltpu.VMEM((512, 512), F32)
    picked_part = pltpu.VMEM((512, 128), F32)
    block = pltpu.VMEM((128, 128), F32)
    tile_f32 = pltpu.VMEM((512, tok // TILES), F32)
    tile_bf = pltpu.VMEM((512, tok // TILES), BF)
    pair = pltpu.SemaphoreType.DMA((2,))
    sems = pltpu.SemaphoreType.DMA((TILES,))
    head_sems = pltpu.SemaphoreType.DMA((HEAD_TILES,))
    tail_sems = pltpu.SemaphoreType.DMA((TAIL_TILES,))
    late_sems = pltpu.SemaphoreType.DMA((LATE_TILES,))

    def exchange(value, axis, order=None):
        return lax.all_to_all(
            value, axis, split_axis=0, concat_axis=0, tiled=True, axis_index_groups=order
        )

    def across(value, flip):
        return lax.ppermute(value, "dp", [(rank, rank ^ flip) for rank in range(8)])

    sent = call(
        head_kernel, "head", (tokens, cotangent, inner_one, outer_two), [by_message], [hbm] * 4, [vmem],
        [by_token, by_token, weight, weight, halves_of, halves_of, pair, head_sems, head_sems], 2 * one,
    )[0]
    got = exchange(sent, "mp")
    sent_two, kept = call(
        middle_kernel, "middle", (got, outer_one, inner_two), [pltpu.HBM((32, 32, tok), BF)] * 2, [vmem, hbm, hbm], [hbm] * 2,
        [weight, weight, by_message, pltpu.VMEM((2, 512, tok // TILES), F32), tile_f32, tile_bf, tile_bf, wide, wide, halves_of, halves_of, pair, sems, pltpu.SemaphoreType.DMA], 4 * one,
    )
    got_two = exchange(sent_two, "mp")
    own, near, middle, far = call(
        early_kernel, "early_grads", (kept, outer_one, inner_two, mine),
        [shape((128 * n, 128), F32) for n in (1, 1, 2, 4)], [vmem, hbm, hbm, smem], [vmem] * 4,
        [weight, weight, tile_f32, tile_f32, tile_bf, tile_bf, wide, wide, total, total, picked_part, block, pair], 4 * one,
    )
    halves = across(far, 4)
    quarters = across(middle + halves[256:], 2)
    eighth = across(near + halves[128:256] + quarters[128:], 1)
    got_two = pltpu.with_memory_space_constraint(got_two, pltpu.HBM)
    tokens_here = call(
        fetch_kernel, "fetch", (tokens,), [by_token], [hbm], [vmem], [pltpu.SemaphoreType.DMA], 0
    )[0]
    outer_one_sum = own[:64] + halves[:64] + quarters[:64] + eighth[:64]
    inner_two_sum = own[64:] + halves[64:128] + quarters[64:128] + eighth[64:]
    tokens_here, outer_one_sum, inner_two_sum = lax.optimization_barrier((tokens_here, outer_one_sum, inner_two_sum))
    late = call(
        late_kernel, "late_grads", (got_two, tokens_here, cotangent), [shape((8, 128, 128), BF)], [hbm, vmem, hbm], [vmem],
        [by_message, by_token, total, total, picked_part, block] + [late_sems] * 3, 2 * one,
    )[0]
    late = exchange(late, "dp", [[7 - rank for rank in range(8)]])
    output, input_grad = call(
        tail_kernel, "tail", (got_two, outer_two, inner_one), [pltpu.HBM((tok, 512), BF)] * 2, [hbm] * 3, [hbm] * 2,
        [by_message, by_token, by_token, weight, weight, wide, wide, pair] + [tail_sems] * 3, 2 * one,
    )
    return (
        output,
        input_grad,
        jnp.sum(late[:, 64:], axis=0, dtype=F32).reshape(4, 16, 128),
        outer_one_sum.reshape(4, 16, 128),
        inner_two_sum.reshape(4, 16, 128),
        jnp.sum(late[:, :64], axis=0, dtype=F32).reshape(4, 16, 128),
    )


def solution(mesh):
    placed = (
        P("dp", "mp"),
        P("mp", None, None),
        P("mp", None, None),
        P("mp", None, None),
        P("mp", None, None),
        P("dp", "mp"),
    )
    return jax.shard_map(
        body,
        mesh=mesh,
        in_specs=placed,
        out_specs=(
            P("dp", "mp"),
            P("dp", "mp"),
            P("mp", "dp", None),
            P("mp", "dp", None),
            P("mp", "dp", None),
            P("mp", "dp", None),
        ),
        check_vma=False,
    )
```

```python
import jax
import jax.numpy as jnp
from jax import lax
from jax.experimental import pallas as pl
from jax.experimental.pallas import tpu as pltpu
from jax.sharding import PartitionSpec as P

BF = jnp.bfloat16
F32 = jnp.float32
GELU_SCALE = 0.7978845608028654
GELU_CUBE = 0.044715
HEAD_TILES = 1
TILES = 4
LATE_TILES = 4
TAIL_TILES = 2
ROWS = 64


def dot(left, right, left_dim, right_dim):
    return lax.dot_general(
        left, right, (((left_dim,), (right_dim,)), ((), ())), preferred_element_type=F32
    )


def one_hot(shape, place):
    row = lax.broadcasted_iota(jnp.int32, shape, 0)
    col = lax.broadcasted_iota(jnp.int32, shape, 1)
    return place(row, col).astype(F32).astype(BF)


def fill_first(weight_ref, pair_ref):
    for block in range(4):
        at = block % 2
        spread = one_hot((256, 128), lambda row, col: row == 2 * col + at)
        pair_ref[block // 2, :, 128 * at:128 * at + 128] = dot(spread, weight_ref[block], 1, 1).astype(BF)


def fill_second(weight_ref, pair_ref):
    for block in range(4):
        at = block % 2
        spread = one_hot((256, 128), lambda row, col: row == 8 * (col // 4) + 4 * at + col % 4)
        pair_ref[block // 2, :, 128 * at:128 * at + 128] = dot(spread, weight_ref[block], 1, 0).astype(BF)


def outer_spread(block):
    def place(row, col):
        b = col % 4
        return row == 16 * (col // 4) + 8 * (b // 2) + 2 * block + b % 2

    return one_hot((512, 128), place)


def fill_outer(weight_ref, wide_ref):
    for block in range(4):
        wide_ref[:, 128 * block:128 * block + 128] = dot(outer_spread(block), weight_ref[block], 1, 0).astype(BF)


def fill_outer_t(weight_ref, wide_ref):
    for block in range(4):
        wide_ref[128 * block:128 * block + 128, :] = dot(weight_ref[block], outer_spread(block), 0, 1).astype(BF)


def fill_inner(weight_ref, wide_ref):
    for block in range(4):
        spread = one_hot((128, 512), lambda row, col: col == 4 * row + block)
        wide_ref[128 * block:128 * block + 128, :] = dot(weight_ref[block], spread, 1, 0).astype(BF)


def fill_inner_t(weight_ref, wide_ref):
    for block in range(4):
        spread = one_hot((512, 128), lambda row, col: row == 4 * col + block)
        wide_ref[:, 128 * block:128 * block + 128] = dot(spread, weight_ref[block], 1, 1).astype(BF)


def paired(pair_ref, values, right_dim):
    halves = []
    for half in range(2):
        part = values(slice(256 * half, 256 * half + 256))
        product = dot(pair_ref[half], part, 1, right_dim)
        halves.append(product.reshape(32, 8, product.shape[1]))
    return jnp.concatenate(halves, axis=1).astype(BF)


def rows(value):
    return value.reshape(512, value.shape[-1])


def copies(source, target, sems, tile, axis):
    out = []
    for i in range(source.shape[axis] // tile):
        at = (slice(None),) * axis + (pl.ds(tile * i, tile),)
        out.append(pltpu.make_async_copy(source.at[at], target.at[at], sems.at[i]))
    return out


def begin(many):
    for copy in many:
        copy.start()


def finish(many):
    for copy in many:
        copy.wait()


def load(pairs, sems):
    out = [pltpu.make_async_copy(source, target, sems.at[i]) for i, (source, target) in enumerate(pairs)]
    begin(out)
    return out


def head_kernel(
    x_hbm, g_hbm, inner_hbm, outer_hbm, sent_ref,
    x_buf, g_buf, inner_buf, outer_buf, inner_pair, outer_pair, weight_sems, x_sems, g_sems,
):
    tile = x_buf.shape[0] // HEAD_TILES
    weights = load([(inner_hbm, inner_buf), (outer_hbm, outer_buf)], weight_sems)
    x_copies = copies(x_hbm, x_buf, x_sems, tile, 0)
    g_copies = copies(g_hbm, g_buf, g_sems, tile, 0)
    begin(x_copies)
    begin(g_copies)
    finish(weights)
    fill_first(inner_buf, inner_pair)
    fill_second(outer_buf, outer_pair)
    for part, pair_ref, buf, arriving in ((0, inner_pair, x_buf, x_copies), (1, outer_pair, g_buf, g_copies)):
        for i in range(HEAD_TILES):
            arriving[i].wait()
            lanes = slice(tile * i, tile * i + tile)
            sent_ref[:, 16 * part:16 * part + 16, lanes] = paired(pair_ref, lambda at: buf[lanes, at], 1)


def activate(pre_ref, hidden_ref, grad_hidden_ref, grad_pre_ref):
    for top in range(0, 512, ROWS):
        band = slice(top, top + ROWS)
        pre = pre_ref[band, :]
        square = pre * pre
        bent = jnp.tanh(pre * (GELU_SCALE + (GELU_SCALE * GELU_CUBE) * square))
        half = 0.5 + 0.5 * bent
        hidden_ref[band, :] = (pre * half).astype(BF)
        rise = 0.5 * GELU_SCALE + (1.5 * GELU_SCALE * GELU_CUBE) * square
        slope = half + pre * (1.0 - bent * bent) * rise
        grad_pre_ref[band, :] = (grad_hidden_ref[band, :] * slope).astype(BF)


def middle_kernel(
    got_ref, outer_hbm, inner_hbm, sent_hbm, kept_hbm,
    outer_buf, inner_buf, sent_buf, pre_ref, grad_hidden_ref, hidden_ref, grad_pre_ref,
    outer_wide_t, inner_wide, inner_pair, outer_pair, weight_sems, first_sems, second_sems, kept_sem,
):
    tile = got_ref.shape[2] // TILES
    outer_copy, inner_copy = load([(outer_hbm, outer_buf), (inner_hbm, inner_buf)], weight_sems)
    kept_copy = pltpu.make_async_copy(got_ref, kept_hbm, kept_sem)
    kept_copy.start()
    first_stores, second_stores = (
        copies(sent_buf.at[:, band, :], sent_hbm.at[:, band, :], sems, tile, 2)
        for band, sems in ((pl.ds(0, 16), first_sems), (pl.ds(16, 16), second_sems))
    )
    outer_copy.wait()
    fill_outer_t(outer_buf, outer_wide_t)
    fill_second(outer_buf, outer_pair)
    inner_copy.wait()
    fill_first(inner_buf, inner_pair)
    fill_inner(inner_buf, inner_wide)
    def lanes(i):
        return slice(tile * i, tile * i + tile)

    def pre_act(i):
        pre_ref[i % 2] = dot(outer_wide_t[...], rows(got_ref[:, 0:16, lanes(i)]), 1, 0)

    pre_act(0)
    for i in range(TILES):
        grad_hidden_ref[...] = dot(inner_wide[...], rows(got_ref[:, 16:32, lanes(i)]), 1, 0)
        if i + 1 < TILES:
            pre_act(i + 1)
        activate(pre_ref.at[i % 2], hidden_ref, grad_hidden_ref, grad_pre_ref)
        sent_buf[:, 0:16, lanes(i)] = paired(inner_pair, lambda at: hidden_ref[at, :], 0)
        first_stores[i].start()
        sent_buf[:, 16:32, lanes(i)] = paired(outer_pair, lambda at: grad_pre_ref[at, :], 0)
        second_stores[i].start()
    finish(first_stores)
    finish(second_stores)
    kept_copy.wait()


def picked(total_ref, forward):
    row = lax.broadcasted_iota(jnp.int32, (512, 128), 0)
    mine = (row // 2) % 4 if forward else row % 4
    value = total_ref[:, 0:128]
    for block in range(1, 4):
        value = jnp.where(mine == block, total_ref[:, 128 * block:128 * block + 128], value)
    return value


def spread_out(block_ref, slots, at):
    for rank, out_ref in slots:
        first_row = 16 * rank if isinstance(rank, int) else pl.multiple_of(16 * rank, 16)
        out_ref[at:at + 16, :] = block_ref[pl.ds(first_row, 16), :].astype(out_ref.dtype)


def write_outer(total_ref, picked_ref, block_ref, slots, at):
    picked_ref[...] = picked(total_ref, True)
    for j in range(4):
        for b in range(4):
            row = 8 * (b // 2) + 2 * j + b % 2
            block_ref[pl.ds(b, 32, stride=4), :] = picked_ref[pl.ds(row, 32, stride=16), :]
        spread_out(block_ref, slots, at + 16 * j)


def write_inner(total_ref, picked_ref, block_ref, slots, at):
    picked_ref[...] = picked(total_ref, False)
    for b in range(4):
        block_ref[...] = picked_ref[pl.ds(b, 128, stride=4), :].T
        spread_out(block_ref, slots, at + 16 * b)


def add(total_ref, value, start):
    if start:
        total_ref[...] = value
    else:
        total_ref[...] += value


def early_kernel(
    got_ref, outer_hbm, inner_hbm, mine_ref, own_ref, near_ref, middle_ref, far_ref,
    outer_buf, inner_buf, pre_ref, grad_hidden_ref, hidden_ref, grad_pre_ref, outer_wide_t, inner_wide,
    outer_total, inner_total, picked_ref, block_ref, weight_sems,
):
    tile = got_ref.shape[2] // TILES
    finish(load([(outer_hbm, outer_buf), (inner_hbm, inner_buf)], weight_sems))
    fill_outer_t(outer_buf, outer_wide_t)
    fill_inner(inner_buf, inner_wide)
    for i in range(TILES):
        lanes = slice(tile * i, tile * i + tile)
        first_perm = rows(got_ref[:, 0:16, lanes])
        grad_mid = rows(got_ref[:, 16:32, lanes])
        pre_ref[...] = dot(outer_wide_t[...], first_perm, 1, 0)
        grad_hidden_ref[...] = dot(inner_wide[...], grad_mid, 1, 0)
        activate(pre_ref, hidden_ref, grad_hidden_ref, grad_pre_ref)
        add(outer_total, dot(first_perm, grad_pre_ref[...], 1, 1), i == 0)
        add(inner_total, dot(grad_mid, hidden_ref[...], 1, 1), i == 0)
    slabs = [(own_ref, 0), (near_ref, 0), (middle_ref, 0), (middle_ref, 128)] + [(far_ref, 128 * i) for i in range(4)]
    slots = [(mine_ref[0] ^ i, ref.at[pl.ds(row, 128), :]) for i, (ref, row) in enumerate(slabs)]
    write_outer(outer_total, picked_ref, block_ref, slots, 0)
    write_inner(inner_total, picked_ref, block_ref, slots, 64)


def fetch_kernel(x_hbm, x_ref, sem):
    copy = pltpu.make_async_copy(x_hbm, x_ref, sem)
    copy.start()
    copy.wait()


def late_kernel(
    got_hbm, x_ref, g_hbm, out_ref,
    got_buf, g_buf, outer_total, inner_total, picked_ref, block_ref, second_sems, grad_sems, g_sems,
):
    tile = g_buf.shape[0] // LATE_TILES
    slots = [(rank, out_ref.at[7 - rank]) for rank in range(8)]
    g_copies = copies(g_hbm, g_buf, g_sems, tile, 0)
    second = copies(got_hbm.at[:, 0:16, :], got_buf.at[:, 0:16, :], second_sems, tile, 2)
    grad = copies(got_hbm.at[:, 16:32, :], got_buf.at[:, 16:32, :], grad_sems, tile, 2)
    begin(grad)
    for i in range(LATE_TILES):
        begin([second[i], g_copies[i]])
    for i in range(LATE_TILES):
        lanes = slice(tile * i, tile * i + tile)
        grad[i].wait()
        add(inner_total, dot(rows(got_buf[:, 16:32, lanes]), x_ref[lanes, :], 1, 0), i == 0)
    write_inner(inner_total, picked_ref, block_ref, slots, 64)
    for i in range(LATE_TILES):
        lanes = slice(tile * i, tile * i + tile)
        finish([second[i], g_copies[i]])
        add(outer_total, dot(rows(got_buf[:, 0:16, lanes]), g_buf[lanes, :], 1, 0), i == 0)
    write_outer(outer_total, picked_ref, block_ref, slots, 0)


def tail_kernel(
    got_hbm, outer_hbm, inner_hbm, output_hbm, input_grad_hbm,
    got_buf, output_buf, input_grad_buf, outer_buf, inner_buf, outer_wide, inner_wide,
    weight_sems, got_sems, output_sems, input_grad_sems,
):
    tile = output_buf.shape[0] // TAIL_TILES
    weights = load([(outer_hbm, outer_buf), (inner_hbm, inner_buf)], weight_sems)
    loads = copies(got_hbm, got_buf, got_sems, tile, 2)
    begin(loads)
    finish(weights)
    fill_outer(outer_buf, outer_wide)
    fill_inner_t(inner_buf, inner_wide)
    output_stores = copies(output_buf, output_hbm, output_sems, tile, 0)
    input_grad_stores = copies(input_grad_buf, input_grad_hbm, input_grad_sems, tile, 0)
    for i in range(TAIL_TILES):
        lanes = slice(tile * i, tile * i + tile)
        loads[i].wait()
        output_buf[lanes, :] = dot(rows(got_buf[:, 0:16, lanes]), outer_wide[...], 0, 0).astype(BF)
        output_stores[i].start()
        input_grad_buf[lanes, :] = dot(rows(got_buf[:, 16:32, lanes]), inner_wide[...], 0, 0).astype(BF)
        input_grad_stores[i].start()
    finish(output_stores)
    finish(input_grad_stores)


def call(kernel, name, args, outs, specs, out_specs, scratch, flops):
    moved = 2 * sum(a.size for a in args)
    return pl.pallas_call(
        kernel,
        in_specs=specs,
        out_specs=out_specs,
        out_shape=outs,
        scratch_shapes=scratch,
        name=name,
        cost_estimate=pl.CostEstimate(flops=flops, bytes_accessed=moved, transcendentals=0),
        compiler_params=pltpu.CompilerParams(vmem_limit_bytes=24 * 1024 * 1024),
    )(*args)


def body(tokens, inner_one, outer_one, inner_two, outer_two, cotangent):
    tok = tokens.shape[0]
    one = 2 * tok * 512 * 512
    mine = lax.axis_index("dp").astype(jnp.int32).reshape(1)
    tokens, cotangent, inner_one, outer_one, inner_two, outer_two = (
        pltpu.with_memory_space_constraint(value, pltpu.HBM)
        for value in (tokens, cotangent, inner_one, outer_one, inner_two, outer_two)
    )
    shape = jax.ShapeDtypeStruct
    hbm = pl.BlockSpec(memory_space=pltpu.HBM)
    vmem = pl.BlockSpec(memory_space=pltpu.VMEM)
    smem = pl.BlockSpec(memory_space=pltpu.SMEM)
    weight = pltpu.VMEM((4, 128, 128), BF)
    by_token = pltpu.VMEM((tok, 512), BF)
    by_message = pltpu.VMEM((32, 32, tok), BF)
    wide = pltpu.VMEM((512, 512), BF)
    halves_of = pltpu.VMEM((2, 256, 256), BF)
    total = pltpu.VMEM((512, 512), F32)
    picked_part = pltpu.VMEM((512, 128), F32)
    block = pltpu.VMEM((128, 128), F32)
    tile_f32 = pltpu.VMEM((512, tok // TILES), F32)
    tile_bf = pltpu.VMEM((512, tok // TILES), BF)
    pair = pltpu.SemaphoreType.DMA((2,))
    sems = pltpu.SemaphoreType.DMA((TILES,))
    head_sems = pltpu.SemaphoreType.DMA((HEAD_TILES,))
    tail_sems = pltpu.SemaphoreType.DMA((TAIL_TILES,))
    late_sems = pltpu.SemaphoreType.DMA((LATE_TILES,))

    def exchange(value, axis, order=None):
        return lax.all_to_all(
            value, axis, split_axis=0, concat_axis=0, tiled=True, axis_index_groups=order
        )

    def across(value, flip):
        return lax.ppermute(value, "dp", [(rank, rank ^ flip) for rank in range(8)])

    sent = call(
        head_kernel, "head", (tokens, cotangent, inner_one, outer_two), [by_message], [hbm] * 4, [vmem],
        [by_token, by_token, weight, weight, halves_of, halves_of, pair, head_sems, head_sems], 2 * one,
    )[0]
    got = exchange(sent, "mp")
    sent_two, kept = call(
        middle_kernel, "middle", (got, outer_one, inner_two), [pltpu.HBM((32, 32, tok), BF)] * 2, [vmem, hbm, hbm], [hbm] * 2,
        [weight, weight, by_message, pltpu.VMEM((2, 512, tok // TILES), F32), tile_f32, tile_bf, tile_bf, wide, wide, halves_of, halves_of, pair, sems, sems, pltpu.SemaphoreType.DMA], 4 * one,
    )
    got_two = exchange(sent_two, "mp")
    own, near, middle, far = call(
        early_kernel, "early_grads", (kept, outer_one, inner_two, mine),
        [shape((128 * n, 128), F32) for n in (1, 1, 2, 4)], [vmem, hbm, hbm, smem], [vmem] * 4,
        [weight, weight, tile_f32, tile_f32, tile_bf, tile_bf, wide, wide, total, total, picked_part, block, pair], 4 * one,
    )
    halves = across(far, 4)
    quarters = across(middle + halves[256:], 2)
    eighth = across(near + halves[128:256] + quarters[128:], 1)
    got_two = pltpu.with_memory_space_constraint(got_two, pltpu.HBM)
    tokens_here = call(
        fetch_kernel, "fetch", (tokens,), [by_token], [hbm], [vmem], [pltpu.SemaphoreType.DMA], 0
    )[0]
    outer_one_sum = own[:64] + halves[:64] + quarters[:64] + eighth[:64]
    inner_two_sum = own[64:] + halves[64:128] + quarters[64:128] + eighth[64:]
    tokens_here, outer_one_sum, inner_two_sum = lax.optimization_barrier((tokens_here, outer_one_sum, inner_two_sum))
    late = call(
        late_kernel, "late_grads", (got_two, tokens_here, cotangent), [shape((8, 128, 128), BF)], [hbm, vmem, hbm], [vmem],
        [by_message, by_token, total, total, picked_part, block] + [late_sems] * 3, 2 * one,
    )[0]
    late = exchange(late, "dp", [[7 - rank for rank in range(8)]])
    output, input_grad = call(
        tail_kernel, "tail", (got_two, outer_two, inner_one), [pltpu.HBM((tok, 512), BF)] * 2, [hbm] * 3, [hbm] * 2,
        [by_message, by_token, by_token, weight, weight, wide, wide, pair] + [tail_sems] * 3, 2 * one,
    )
    return (
        output,
        input_grad,
        jnp.sum(late[:, 64:], axis=0, dtype=F32).reshape(4, 16, 128),
        outer_one_sum.reshape(4, 16, 128),
        inner_two_sum.reshape(4, 16, 128),
        jnp.sum(late[:, :64], axis=0, dtype=F32).reshape(4, 16, 128),
    )


def solution(mesh):
    placed = (
        P("dp", "mp"),
        P("mp", None, None),
        P("mp", None, None),
        P("mp", None, None),
        P("mp", None, None),
        P("dp", "mp"),
    )
    return jax.shard_map(
        body,
        mesh=mesh,
        in_specs=placed,
        out_specs=(
            P("dp", "mp"),
            P("dp", "mp"),
            P("mp", "dp", None),
            P("mp", "dp", None),
            P("mp", "dp", None),
            P("mp", "dp", None),
        ),
        check_vma=False,
    )
```

```python
import jax
import jax.numpy as jnp
from jax import lax
from jax.experimental import pallas as pl
from jax.experimental.pallas import tpu as pltpu
from jax.sharding import PartitionSpec as P

BF = jnp.bfloat16
F32 = jnp.float32
GELU_SCALE = 0.7978845608028654
GELU_CUBE = 0.044715
HEAD_TILES = 1
TILES = 4
LATE_TILES = 2
TAIL_TILES = 2
ROWS = 64


def dot(left, right, left_dim, right_dim):
    return lax.dot_general(
        left, right, (((left_dim,), (right_dim,)), ((), ())), preferred_element_type=F32
    )


def one_hot(shape, place):
    row = lax.broadcasted_iota(jnp.int32, shape, 0)
    col = lax.broadcasted_iota(jnp.int32, shape, 1)
    return place(row, col).astype(F32).astype(BF)


def fill_first(weight_ref, pair_ref):
    for block in range(4):
        at = block % 2
        spread = one_hot((256, 128), lambda row, col: row == 2 * col + at)
        pair_ref[block // 2, :, 128 * at:128 * at + 128] = dot(spread, weight_ref[block], 1, 1).astype(BF)


def fill_second(weight_ref, pair_ref):
    for block in range(4):
        at = block % 2
        spread = one_hot((256, 128), lambda row, col: row == 8 * (col // 4) + 4 * at + col % 4)
        pair_ref[block // 2, :, 128 * at:128 * at + 128] = dot(spread, weight_ref[block], 1, 0).astype(BF)


def outer_spread(block):
    def place(row, col):
        b = col % 4
        return row == 16 * (col // 4) + 8 * (b // 2) + 2 * block + b % 2

    return one_hot((512, 128), place)


def fill_outer(weight_ref, wide_ref):
    for block in range(4):
        wide_ref[:, 128 * block:128 * block + 128] = dot(outer_spread(block), weight_ref[block], 1, 0).astype(BF)


def fill_outer_t(weight_ref, wide_ref):
    for block in range(4):
        wide_ref[128 * block:128 * block + 128, :] = dot(weight_ref[block], outer_spread(block), 0, 1).astype(BF)


def fill_inner(weight_ref, wide_ref):
    for block in range(4):
        spread = one_hot((128, 512), lambda row, col: col == 4 * row + block)
        wide_ref[128 * block:128 * block + 128, :] = dot(weight_ref[block], spread, 1, 0).astype(BF)


def fill_inner_t(weight_ref, wide_ref):
    for block in range(4):
        spread = one_hot((512, 128), lambda row, col: row == 4 * col + block)
        wide_ref[:, 128 * block:128 * block + 128] = dot(spread, weight_ref[block], 1, 1).astype(BF)


def paired(pair_ref, values, right_dim):
    halves = []
    for half in range(2):
        part = values(slice(256 * half, 256 * half + 256))
        product = dot(pair_ref[half], part, 1, right_dim)
        halves.append(product.reshape(32, 8, product.shape[1]))
    return jnp.concatenate(halves, axis=1).astype(BF)


def rows(value):
    return value.reshape(512, value.shape[-1])


def copies(source, target, sems, tile, axis):
    out = []
    for i in range(source.shape[axis] // tile):
        at = (slice(None),) * axis + (pl.ds(tile * i, tile),)
        out.append(pltpu.make_async_copy(source.at[at], target.at[at], sems.at[i]))
    return out


def begin(many):
    for copy in many:
        copy.start()


def finish(many):
    for copy in many:
        copy.wait()


def load(pairs, sems):
    out = [pltpu.make_async_copy(source, target, sems.at[i]) for i, (source, target) in enumerate(pairs)]
    begin(out)
    return out


def head_kernel(
    x_hbm, g_hbm, inner_hbm, outer_hbm, sent_ref,
    x_buf, g_buf, inner_buf, outer_buf, inner_pair, outer_pair, weight_sems, x_sems, g_sems,
):
    tile = x_buf.shape[0] // HEAD_TILES
    weights = load([(inner_hbm, inner_buf), (outer_hbm, outer_buf)], weight_sems)
    x_copies = copies(x_hbm, x_buf, x_sems, tile, 0)
    g_copies = copies(g_hbm, g_buf, g_sems, tile, 0)
    begin(x_copies)
    begin(g_copies)
    finish(weights)
    fill_first(inner_buf, inner_pair)
    fill_second(outer_buf, outer_pair)
    for part, pair_ref, buf, arriving in ((0, inner_pair, x_buf, x_copies), (1, outer_pair, g_buf, g_copies)):
        for i in range(HEAD_TILES):
            arriving[i].wait()
            lanes = slice(tile * i, tile * i + tile)
            sent_ref[:, 16 * part:16 * part + 16, lanes] = paired(pair_ref, lambda at: buf[lanes, at], 1)


def activate(pre_ref, hidden_ref, grad_hidden_ref, grad_pre_ref):
    for top in range(0, 512, ROWS):
        band = slice(top, top + ROWS)
        pre = pre_ref[band, :]
        square = pre * pre
        bent = jnp.tanh(pre * (GELU_SCALE + (GELU_SCALE * GELU_CUBE) * square))
        half = 0.5 + 0.5 * bent
        hidden_ref[band, :] = (pre * half).astype(BF)
        rise = 0.5 * GELU_SCALE + (1.5 * GELU_SCALE * GELU_CUBE) * square
        slope = half + pre * (1.0 - bent * bent) * rise
        grad_pre_ref[band, :] = (grad_hidden_ref[band, :] * slope).astype(BF)


def middle_kernel(
    got_ref, outer_hbm, inner_hbm, sent_hbm, kept_hbm,
    outer_buf, inner_buf, sent_buf, pre_ref, grad_hidden_ref, hidden_ref, grad_pre_ref,
    outer_wide_t, inner_wide, inner_pair, outer_pair, weight_sems, sent_sems, kept_sem,
):
    tile = got_ref.shape[2] // TILES
    outer_copy, inner_copy = load([(outer_hbm, outer_buf), (inner_hbm, inner_buf)], weight_sems)
    kept_copy = pltpu.make_async_copy(got_ref, kept_hbm, kept_sem)
    kept_copy.start()
    sent_stores = copies(sent_buf, sent_hbm, sent_sems, tile, 2)
    outer_copy.wait()
    fill_outer_t(outer_buf, outer_wide_t)
    fill_second(outer_buf, outer_pair)
    inner_copy.wait()
    fill_first(inner_buf, inner_pair)
    fill_inner(inner_buf, inner_wide)
    def lanes(i):
        return slice(tile * i, tile * i + tile)

    def pre_act(i):
        pre_ref[i % 2] = dot(outer_wide_t[...], rows(got_ref[:, 0:16, lanes(i)]), 1, 0)

    pre_act(0)
    for i in range(TILES):
        grad_hidden_ref[...] = dot(inner_wide[...], rows(got_ref[:, 16:32, lanes(i)]), 1, 0)
        if i + 1 < TILES:
            pre_act(i + 1)
        activate(pre_ref.at[i % 2], hidden_ref, grad_hidden_ref, grad_pre_ref)
        sent_buf[:, 0:16, lanes(i)] = paired(inner_pair, lambda at: hidden_ref[at, :], 0)
        sent_buf[:, 16:32, lanes(i)] = paired(outer_pair, lambda at: grad_pre_ref[at, :], 0)
        sent_stores[i].start()
    finish(sent_stores)
    kept_copy.wait()


def picked(total_ref, forward):
    row = lax.broadcasted_iota(jnp.int32, (512, 128), 0)
    mine = (row // 2) % 4 if forward else row % 4
    value = total_ref[:, 0:128]
    for block in range(1, 4):
        value = jnp.where(mine == block, total_ref[:, 128 * block:128 * block + 128], value)
    return value


def spread_out(block_ref, slots, at):
    for rank, out_ref in slots:
        first_row = 16 * rank if isinstance(rank, int) else pl.multiple_of(16 * rank, 16)
        out_ref[at:at + 16, :] = block_ref[pl.ds(first_row, 16), :].astype(out_ref.dtype)


def write_outer(total_ref, picked_ref, block_ref, slots, at):
    picked_ref[...] = picked(total_ref, True)
    for j in range(4):
        for b in range(4):
            row = 8 * (b // 2) + 2 * j + b % 2
            block_ref[pl.ds(b, 32, stride=4), :] = picked_ref[pl.ds(row, 32, stride=16), :]
        spread_out(block_ref, slots, at + 16 * j)


def write_inner(total_ref, picked_ref, block_ref, slots, at):
    picked_ref[...] = picked(total_ref, False)
    for b in range(4):
        block_ref[...] = picked_ref[pl.ds(b, 128, stride=4), :].T
        spread_out(block_ref, slots, at + 16 * b)


def add(total_ref, value, start):
    if start:
        total_ref[...] = value
    else:
        total_ref[...] += value


def early_kernel(
    got_ref, outer_hbm, inner_hbm, mine_ref, own_ref, near_ref, middle_ref, far_ref,
    outer_buf, inner_buf, pre_ref, grad_hidden_ref, hidden_ref, grad_pre_ref, outer_wide_t, inner_wide,
    outer_total, inner_total, picked_ref, block_ref, weight_sems,
):
    tile = got_ref.shape[2] // TILES
    finish(load([(outer_hbm, outer_buf), (inner_hbm, inner_buf)], weight_sems))
    fill_outer_t(outer_buf, outer_wide_t)
    fill_inner(inner_buf, inner_wide)
    for i in range(TILES):
        lanes = slice(tile * i, tile * i + tile)
        first_perm = rows(got_ref[:, 0:16, lanes])
        grad_mid = rows(got_ref[:, 16:32, lanes])
        pre_ref[...] = dot(outer_wide_t[...], first_perm, 1, 0)
        grad_hidden_ref[...] = dot(inner_wide[...], grad_mid, 1, 0)
        activate(pre_ref, hidden_ref, grad_hidden_ref, grad_pre_ref)
        add(outer_total, dot(first_perm, grad_pre_ref[...], 1, 1), i == 0)
        add(inner_total, dot(grad_mid, hidden_ref[...], 1, 1), i == 0)
    slabs = [(own_ref, 0), (near_ref, 0), (middle_ref, 0), (middle_ref, 128)] + [(far_ref, 128 * i) for i in range(4)]
    slots = [(mine_ref[0] ^ i, ref.at[pl.ds(row, 128), :]) for i, (ref, row) in enumerate(slabs)]
    write_outer(outer_total, picked_ref, block_ref, slots, 0)
    write_inner(inner_total, picked_ref, block_ref, slots, 64)


def fetch_kernel(x_hbm, x_ref, sem):
    copy = pltpu.make_async_copy(x_hbm, x_ref, sem)
    copy.start()
    copy.wait()


def late_kernel(
    got_hbm, x_ref, g_hbm, out_ref,
    got_buf, g_buf, outer_total, inner_total, picked_ref, block_ref, second_sems, grad_sems, g_sems,
):
    tile = g_buf.shape[0] // LATE_TILES
    slots = [(rank, out_ref.at[7 - rank]) for rank in range(8)]
    g_copies = copies(g_hbm, g_buf, g_sems, tile, 0)
    second = copies(got_hbm.at[:, 0:16, :], got_buf.at[:, 0:16, :], second_sems, tile, 2)
    grad = copies(got_hbm.at[:, 16:32, :], got_buf.at[:, 16:32, :], grad_sems, tile, 2)
    begin(grad)
    for i in range(LATE_TILES):
        begin([second[i], g_copies[i]])
    for i in range(LATE_TILES):
        lanes = slice(tile * i, tile * i + tile)
        grad[i].wait()
        add(inner_total, dot(rows(got_buf[:, 16:32, lanes]), x_ref[lanes, :], 1, 0), i == 0)
    write_inner(inner_total, picked_ref, block_ref, slots, 64)
    for i in range(LATE_TILES):
        lanes = slice(tile * i, tile * i + tile)
        finish([second[i], g_copies[i]])
        add(outer_total, dot(rows(got_buf[:, 0:16, lanes]), g_buf[lanes, :], 1, 0), i == 0)
    write_outer(outer_total, picked_ref, block_ref, slots, 0)


def tail_kernel(
    got_hbm, outer_hbm, inner_hbm, output_hbm, input_grad_hbm,
    got_buf, output_buf, input_grad_buf, outer_buf, inner_buf, outer_wide, inner_wide,
    weight_sems, got_sems, output_sems, input_grad_sems,
):
    tile = output_buf.shape[0] // TAIL_TILES
    weights = load([(outer_hbm, outer_buf), (inner_hbm, inner_buf)], weight_sems)
    loads = copies(got_hbm, got_buf, got_sems, tile, 2)
    begin(loads)
    finish(weights)
    fill_outer(outer_buf, outer_wide)
    fill_inner_t(inner_buf, inner_wide)
    output_stores = copies(output_buf, output_hbm, output_sems, tile, 0)
    input_grad_stores = copies(input_grad_buf, input_grad_hbm, input_grad_sems, tile, 0)
    for i in range(TAIL_TILES):
        lanes = slice(tile * i, tile * i + tile)
        loads[i].wait()
        output_buf[lanes, :] = dot(rows(got_buf[:, 0:16, lanes]), outer_wide[...], 0, 0).astype(BF)
        output_stores[i].start()
        input_grad_buf[lanes, :] = dot(rows(got_buf[:, 16:32, lanes]), inner_wide[...], 0, 0).astype(BF)
        input_grad_stores[i].start()
    finish(output_stores)
    finish(input_grad_stores)


def call(kernel, name, args, outs, specs, out_specs, scratch, flops):
    moved = 2 * sum(a.size for a in args)
    return pl.pallas_call(
        kernel,
        in_specs=specs,
        out_specs=out_specs,
        out_shape=outs,
        scratch_shapes=scratch,
        name=name,
        cost_estimate=pl.CostEstimate(flops=flops, bytes_accessed=moved, transcendentals=0),
        compiler_params=pltpu.CompilerParams(vmem_limit_bytes=24 * 1024 * 1024),
    )(*args)


def body(tokens, inner_one, outer_one, inner_two, outer_two, cotangent):
    tok = tokens.shape[0]
    one = 2 * tok * 512 * 512
    mine = lax.axis_index("dp").astype(jnp.int32).reshape(1)
    tokens, cotangent, inner_one, outer_one, inner_two, outer_two = (
        pltpu.with_memory_space_constraint(value, pltpu.HBM)
        for value in (tokens, cotangent, inner_one, outer_one, inner_two, outer_two)
    )
    shape = jax.ShapeDtypeStruct
    hbm = pl.BlockSpec(memory_space=pltpu.HBM)
    vmem = pl.BlockSpec(memory_space=pltpu.VMEM)
    smem = pl.BlockSpec(memory_space=pltpu.SMEM)
    weight = pltpu.VMEM((4, 128, 128), BF)
    by_token = pltpu.VMEM((tok, 512), BF)
    by_message = pltpu.VMEM((32, 32, tok), BF)
    wide = pltpu.VMEM((512, 512), BF)
    halves_of = pltpu.VMEM((2, 256, 256), BF)
    total = pltpu.VMEM((512, 512), F32)
    picked_part = pltpu.VMEM((512, 128), F32)
    block = pltpu.VMEM((128, 128), F32)
    tile_f32 = pltpu.VMEM((512, tok // TILES), F32)
    tile_bf = pltpu.VMEM((512, tok // TILES), BF)
    pair = pltpu.SemaphoreType.DMA((2,))
    sems = pltpu.SemaphoreType.DMA((TILES,))
    head_sems = pltpu.SemaphoreType.DMA((HEAD_TILES,))
    tail_sems = pltpu.SemaphoreType.DMA((TAIL_TILES,))
    late_sems = pltpu.SemaphoreType.DMA((LATE_TILES,))

    def exchange(value, axis, order=None):
        return lax.all_to_all(
            value, axis, split_axis=0, concat_axis=0, tiled=True, axis_index_groups=order
        )

    def across(value, flip):
        return lax.ppermute(value, "dp", [(rank, rank ^ flip) for rank in range(8)])

    sent = call(
        head_kernel, "head", (tokens, cotangent, inner_one, outer_two), [by_message], [hbm] * 4, [vmem],
        [by_token, by_token, weight, weight, halves_of, halves_of, pair, head_sems, head_sems], 2 * one,
    )[0]
    got = exchange(sent, "mp")
    sent_two, kept = call(
        middle_kernel, "middle", (got, outer_one, inner_two), [pltpu.HBM((32, 32, tok), BF)] * 2, [vmem, hbm, hbm], [hbm] * 2,
        [weight, weight, by_message, pltpu.VMEM((2, 512, tok // TILES), F32), tile_f32, tile_bf, tile_bf, wide, wide, halves_of, halves_of, pair, sems, pltpu.SemaphoreType.DMA], 4 * one,
    )
    got_two = exchange(sent_two, "mp")
    own, near, middle, far = call(
        early_kernel, "early_grads", (kept, outer_one, inner_two, mine),
        [shape((128 * n, 128), F32) for n in (1, 1, 2, 4)], [vmem, hbm, hbm, smem], [vmem] * 4,
        [weight, weight, tile_f32, tile_f32, tile_bf, tile_bf, wide, wide, total, total, picked_part, block, pair], 4 * one,
    )
    halves = across(far, 4)
    quarters = across(middle + halves[256:], 2)
    eighth = across(near + halves[128:256] + quarters[128:], 1)
    got_two = pltpu.with_memory_space_constraint(got_two, pltpu.HBM)
    tokens_here = call(
        fetch_kernel, "fetch", (tokens,), [by_token], [hbm], [vmem], [pltpu.SemaphoreType.DMA], 0
    )[0]
    outer_one_sum = own[:64] + halves[:64] + quarters[:64] + eighth[:64]
    inner_two_sum = own[64:] + halves[64:128] + quarters[64:128] + eighth[64:]
    tokens_here, outer_one_sum, inner_two_sum = lax.optimization_barrier((tokens_here, outer_one_sum, inner_two_sum))
    late = call(
        late_kernel, "late_grads", (got_two, tokens_here, cotangent), [shape((8, 128, 128), BF)], [hbm, vmem, hbm], [vmem],
        [by_message, by_token, total, total, picked_part, block] + [late_sems] * 3, 2 * one,
    )[0]
    late = exchange(late, "dp", [[7 - rank for rank in range(8)]])
    output, input_grad = call(
        tail_kernel, "tail", (got_two, outer_two, inner_one), [pltpu.HBM((tok, 512), BF)] * 2, [hbm] * 3, [hbm] * 2,
        [by_message, by_token, by_token, weight, weight, wide, wide, pair] + [tail_sems] * 3, 2 * one,
    )
    return (
        output,
        input_grad,
        jnp.sum(late[:, 64:], axis=0, dtype=F32).reshape(4, 16, 128),
        outer_one_sum.reshape(4, 16, 128),
        inner_two_sum.reshape(4, 16, 128),
        jnp.sum(late[:, :64], axis=0, dtype=F32).reshape(4, 16, 128),
    )


def solution(mesh):
    placed = (
        P("dp", "mp"),
        P("mp", None, None),
        P("mp", None, None),
        P("mp", None, None),
        P("mp", None, None),
        P("dp", "mp"),
    )
    return jax.shard_map(
        body,
        mesh=mesh,
        in_specs=placed,
        out_specs=(
            P("dp", "mp"),
            P("dp", "mp"),
            P("mp", "dp", None),
            P("mp", "dp", None),
            P("mp", "dp", None),
            P("mp", "dp", None),
        ),
        check_vma=False,
    )
```
